256 devices in a mesh: ev: 32 (over z, y), pol: 8 (over x, core).
Axes of the slice: x: 4, y: 4, z: 8, core: 2. Of those that a mesh axis runs over, the one named last changes fastest.
Arguments:
- ground_up: bfloat16 [1536, 512, 128], P('pol', 'ev'), may hold values from 1.9907951e-05 to 0.0019989014
- loc_deductible: bfloat16 [1536, 128], P('pol'), may hold values from 0 to 0.00029945374
- loc_limit: bfloat16 [1536, 128], P('pol'), may hold values from 0.00049972534 to 0.0014953613
- block_policy: int32 [1536], P('pol'), may hold values from 0 to 511, as said below
- policy_deductible: float32 [512], P('pol'), may hold values from 0.02 to 0.12
- policy_limit: float32 [512], P('pol'), may hold values from 0.05 to 0.2
- policy_share: float32 [512], P('pol'), may hold values from 0.3 to 1
- policy_summary: int32 [512], P('pol'), may hold values from 0 to 31
- occurrence: int32 [512, 64], P('ev'), may hold values from 0 to 32767
Outputs:
- year_loss: float32 [32, 32768], P('pol', 'ev')
The draws below stay inside these ranges and needn't reach their ends.
Inputs may be any that keep to these rules, and one draw needn't show every extreme that they name: `block_policy`: policy q is owned by index q // 64 of pol. Among the 192 blocks held by one index of pol, at most 36 belong to policies of any one owner; in every draw some owner gets exactly 36 blocks from every index of pol.
All inputs are finite; a program needn't handle non-finite values.
Results may differ from the reference program's by a relative error of at most 0.0003.
Values sent between devices are 32-bit elements; how exact they have to be, the bound alone decides.
No kernel may reach another device: no remote copies, remote signals or barrier semaphores. Data moves between devices by JAX's collectives and lax.ppermute only.
A program may use at most 64 MiB of HBM per device.

```python
import math
import jax
import jax.numpy as jnp
from jax import lax

LOC = 128
BLK_DEV = 192
POL_DEV = 64
SUMM = 32
OCC = 64
EVENTS = 512
BLOCKS = 1536
POLICIES = 512
YEARS = 32768
CAP = 36


def draw_block_policy(key, part):
    sources = BLOCKS // BLK_DEV
    owner_total = POLICIES // POL_DEV
    slot_total = owner_total * CAP
    first_key, second_key, third_key, fourth_key = jax.random.split(jax.random.fold_in(key, 7177), 4)
    full_owner = jax.random.randint(first_key, (), 0, owner_total)
    slot_owner = jnp.repeat(jnp.arange(owner_total, dtype=jnp.int32), CAP)
    noise_bits = jax.random.randint(second_key, (sources, slot_total), 0, 1 << 20)
    scores = noise_bits * slot_total + jnp.arange(slot_total, dtype=jnp.int32)[None, :]
    scores = jnp.where(slot_owner[None, :] == full_owner, scores - (1 << 30), scores)
    chosen = jnp.argsort(scores, axis=1, stable=True)[:, :BLK_DEV]
    owners = slot_owner[chosen]
    shuffle_bits = jax.random.randint(third_key, (sources, BLK_DEV), 0, 1 << 20)
    shuffle_scores = shuffle_bits * BLK_DEV + jnp.arange(BLK_DEV, dtype=jnp.int32)[None, :]
    shuffled = jnp.argsort(shuffle_scores, axis=1, stable=True)
    owners = jnp.take_along_axis(owners, shuffled, axis=1)
    local_policy = jax.random.randint(fourth_key, (sources, BLK_DEV), 0, POL_DEV)
    return (owners * POL_DEV + local_policy).reshape(-1).astype(jnp.int32)


def place_ends(entries, key, low, top_value):
    extent = entries.shape
    spot = [jax.random.randint(jax.random.fold_in(key, axis), (), 0, extent[axis]) for axis in range(len(extent))]
    entries = entries.at[tuple(spot)].set(low)
    longest = extent.index(max(extent))
    spot[longest] = (spot[longest] + 1) % extent[longest]
    return entries.at[tuple(spot)].set(top_value)


def level_of(key, shape, cuts, least, high):
    def one(position, shards_of):
        draws = jax.random.uniform(jax.random.fold_in(jax.random.fold_in(key, 6), position), (shards_of,), jnp.float32, least / len(cuts), high / len(cuts))
        return jnp.repeat(jnp.exp(draws), shape[position] // shards_of).reshape((-1,) + (1,) * (len(shape) - position - 1))

    gain = one(*cuts[0])
    for cut in cuts[1:]:
        gain = gain * one(*cut)
    return gain


def setup_inputs(seed: int = 0) -> dict:
    keys = jax.random.split(jax.random.key(seed), 10)
    ground_up = jnp.clip(jnp.exp(math.log(0.0019989014) - 4.609234 * jax.random.uniform(keys[0], (BLOCKS, EVENTS, LOC), jnp.float32) ** level_of(keys[0], (BLOCKS, EVENTS, LOC), ((0, 8), (1, 32)), -0.2, 0.2)), 1.990795135498047e-05, 0.0019989014).astype(jnp.bfloat16)
    loc_deductible = jnp.clip(0.00029945374 * jax.random.uniform(keys[1], (BLOCKS, LOC), jnp.float32) ** level_of(keys[1], (BLOCKS, LOC), ((0, 8),), -0.2, 0.2), 0.0, 0.00029945374).astype(jnp.bfloat16)
    loc_limit = jnp.clip(0.00049972534 + 0.000995636 * jax.random.uniform(keys[2], (BLOCKS, LOC), jnp.float32) ** level_of(keys[2], (BLOCKS, LOC), ((0, 8),), -0.2, 0.2), 0.00049972534, 0.0014953613).astype(jnp.bfloat16)
    block_policy = draw_block_policy(jax.random.fold_in(keys[9], 71), 0)
    policy_deductible = jnp.clip(0.02 + 0.09999999776482582 * jax.random.uniform(keys[4], (POLICIES,), jnp.float32) ** level_of(keys[4], (POLICIES,), ((0, 8),), -0.2, 0.2), 0.02, 0.12)
    policy_limit = jnp.clip(0.05 + 0.15 * jax.random.uniform(keys[5], (POLICIES,), jnp.float32) ** level_of(keys[5], (POLICIES,), ((0, 8),), -0.2, 0.2), 0.05, 0.2)
    policy_share = jnp.clip(0.3 + 0.7 * jax.random.uniform(keys[6], (POLICIES,), jnp.float32) ** level_of(keys[6], (POLICIES,), ((0, 8),), -0.2, 0.2), 0.3, 1.0)
    policy_summary = place_ends(jax.random.randint(keys[7], (POLICIES,), 0, SUMM), jax.random.fold_in(keys[7], 1), 0, SUMM - 1).astype(jnp.int32)
    occurrence = place_ends(jax.random.randint(keys[8], (EVENTS, OCC), 0, YEARS), jax.random.fold_in(keys[8], 1), 0, YEARS - 1).astype(jnp.int32)
    return dict(ground_up=ground_up, loc_deductible=loc_deductible, loc_limit=loc_limit, block_policy=block_policy, policy_deductible=policy_deductible, policy_limit=policy_limit, policy_share=policy_share, policy_summary=policy_summary, occurrence=occurrence)


def block_totals(ground_up, loc_deductible, loc_limit):
    lower = loc_deductible.astype(jnp.float32)[:, None, :]
    upper = loc_limit.astype(jnp.float32)[:, None, :]
    net_loss = jnp.minimum(jnp.maximum(ground_up.astype(jnp.float32) - lower, 0.0), upper)
    return jnp.sum(net_loss, axis=2)


def spread(summary_loss, occurrence, year_total):
    per_event = occurrence.shape[1]
    repeated = jnp.repeat(summary_loss, per_event, axis=0)
    empty = jnp.zeros((summary_loss.shape[1], year_total), jnp.float32)
    return empty.at[:, occurrence.reshape(-1)].add(repeated.T)


def reference(ground_up, loc_deductible, loc_limit, block_policy, policy_deductible, policy_limit, policy_share, policy_summary, occurrence):
    groups = BLOCKS // BLK_DEV
    stacked = (ground_up.reshape(groups, BLK_DEV, EVENTS, LOC), loc_deductible.reshape(groups, BLK_DEV, LOC), loc_limit.reshape(groups, BLK_DEV, LOC))
    totals = lax.map(lambda group_blocks: block_totals(group_blocks[0], group_blocks[1], group_blocks[2]), stacked)
    totals = totals.reshape(BLOCKS, EVENTS)
    membership = (block_policy[:, None] == jnp.arange(POLICIES, dtype=jnp.int32)[None, :]).astype(jnp.float32)
    policy_ground = jnp.dot(totals.T, membership, precision=lax.Precision.HIGHEST, preferred_element_type=jnp.float32)
    policy_losses = policy_share * jnp.minimum(jnp.maximum(policy_ground - policy_deductible, 0.0), policy_limit)
    summary_map = (policy_summary[:, None] == jnp.arange(SUMM, dtype=jnp.int32)[None, :]).astype(jnp.float32)
    summary_loss = jnp.dot(policy_losses, summary_map, precision=lax.Precision.HIGHEST, preferred_element_type=jnp.float32)
    return spread(summary_loss, occurrence, YEARS)
```

```python
import jax
import jax.numpy as jnp
from jax import lax
from jax.experimental import pallas as pl
from jax.experimental.pallas import tpu as pltpu
from jax.sharding import PartitionSpec as P

SUMM_DEV = 4
YR_DEV = 1024
GROUP = 28
SLOT = 7
NT = (((1,), (1,)), ((), ()))
VMEM = pl.BlockSpec(memory_space=pltpu.VMEM)


def two_terms(x):
    high = x.astype(jnp.bfloat16)
    return high, (x - high.astype(jnp.float32)).astype(jnp.bfloat16)


def local_kernel(ground, deduct, limit, owner, pol_ded, pol_lim, pol_share, pol_summ, out, terms, ids, params):
    blocks = ground.shape[0]
    terms[:, 16 * SLOT :, :] = jnp.zeros((GROUP, 128 - 16 * SLOT, 256), jnp.bfloat16)
    for i in range(SLOT):
        first = i * GROUP
        count = min(GROUP, blocks - first)
        lower = deduct[first : first + count].astype(jnp.float32)[:, None, :]
        upper = limit[first : first + count].astype(jnp.float32)[:, None, :]
        net = jnp.minimum(jnp.maximum(ground[first : first + count].astype(jnp.float32) - lower, 0.0), upper)
        high, low = two_terms(net)
        terms[:count, 16 * i : 16 * i + 16, :128] = high
        terms[:count, 16 * i : 16 * i + 16, 128:] = low
        if count < GROUP:
            terms[count:, 16 * i : 16 * i + 16, :] = jnp.zeros((GROUP - count, 16, 256), jnp.bfloat16)

    sub = lax.broadcasted_iota(jnp.int32, (8, 128), 0)
    lane = lax.broadcasted_iota(jnp.int32, (8, 128), 1)
    ids[...] = jnp.full((8, 256), -1.0, jnp.float32)
    ids[0:1, 0:blocks] = owner[...].astype(jnp.float32)
    flat = jnp.broadcast_to(ids[0:1, :], (8, 256))
    rows = jnp.full((8, 128), -1.0, jnp.float32)
    for i in range(SLOT):
        piece = flat if i == 0 else pltpu.roll(flat, 256 - i * GROUP, 1)
        rows = jnp.where(sub == i, piece[:, :128], rows)
    place = (lane == sub + 16 * SLOT).astype(jnp.float32)
    columns = lax.dot_general(
        rows, place, (((0,), (0,)), ((), ())), precision=lax.Precision.HIGHEST, preferred_element_type=jnp.float32
    )

    params[...] = jnp.zeros((8, 128), jnp.float32)
    params[4:5, 0:64] = pol_ded[...]
    params[5:6, 0:64] = pol_lim[...]
    params[6:7, 0:64] = pol_share[...]
    params[7:8, 0:64] = pol_summ[...].astype(jnp.float32)
    own = params[...]
    half = lax.rem(lax.axis_index("pol"), 2)
    own = jnp.where(lane // 64 == half, own + pltpu.roll(own, 64, 1), 0.0)

    ones = jnp.ones((8, 256), jnp.bfloat16)
    tiles = [jnp.zeros((8, 128), jnp.float32) for _ in range(4)]
    for n in range(GROUP // 2):
        weights = terms[2 * n : 2 * n + 2].reshape(256, 256)
        sums = lax.dot_general(ones, weights, NT, preferred_element_type=jnp.float32)
        for half_row in range(2):
            r = 2 * n + half_row
            tiles[r // 8] = jnp.where(sub == r % 8, sums[:, 128 * half_row : 128 * half_row + 128], tiles[r // 8])
    tiles = [tiles[t] + columns[8 * t : 8 * t + 8] for t in range(4)]
    tiles[3] = jnp.where(sub < 4, tiles[3], own)
    for t in range(4):
        for k in range(out.shape[0]):
            out[k, 8 * t : 8 * t + 8, :] = tiles[t]


def policy_kernel(arrived, occurrence, out, years):
    owners = arrived.shape[0]
    policies = 64 * owners
    flat = arrived[...].reshape(owners * 32, 128)
    turned = flat.T
    row = lax.broadcasted_iota(jnp.int32, (1, owners * 32), 1) % 32
    high, low = two_terms(turned[: 16 * SLOT])
    policy = lax.broadcasted_iota(jnp.int32, (policies, owners * 32), 0).astype(jnp.float32)
    total = jnp.zeros((32, policies), jnp.float32)
    for i in range(SLOT):
        ids = jnp.where(row < GROUP, turned[16 * SLOT + i : 16 * SLOT + i + 1], -1.0)
        member = (policy == ids).astype(jnp.bfloat16)
        left = jnp.concatenate([high[16 * i : 16 * i + 16], low[16 * i : 16 * i + 16]], axis=0)
        total = total + lax.dot_general(left, member, NT, preferred_element_type=jnp.float32)
    policy_ground = total[:16] + total[16:]

    pairs = [arrived[2 * k, 24:32, :] + arrived[2 * k + 1, 24:32, :] for k in range(owners // 2)]
    params = jnp.concatenate(pairs, axis=1)
    loss = params[6:7] * jnp.minimum(jnp.maximum(policy_ground - params[4:5], 0.0), params[5:6])
    own = lax.axis_index("pol") * SUMM_DEV
    group = lax.broadcasted_iota(jnp.int32, (128, policies), 0)
    wanted = jnp.where(group < SUMM_DEV, (group + own).astype(jnp.float32), -1.0)
    chosen = (wanted == params[7:8]).astype(jnp.bfloat16)
    high, low = two_terms(loss)
    sums = lax.dot_general(jnp.concatenate([high, low], axis=0), chosen, NT, preferred_element_type=jnp.float32)
    sums = sums[:16] + sums[16:]
    tile = sums[:8] + pltpu.roll(sums[8:], SUMM_DEV, 1)

    own_years = occurrence[...].astype(jnp.float32)
    years[:, 0:64] = own_years[:8]
    years[:, 64:128] = own_years[8:]
    year_tile = years[...]
    for k in range(out.shape[0]):
        out[k, 0:8, :] = tile
        out[k, 8:16, :] = year_tile


def year_kernel(arrived, out, spare):
    base = (lax.axis_index("ev") * YR_DEV).astype(jnp.float32)
    lane = lax.broadcasted_iota(jnp.int32, (8, 128), 1)
    upper_row = lax.broadcasted_iota(jnp.int32, (8, 128), 0).astype(jnp.float32)
    lower_row = lax.broadcasted_iota(jnp.int32, (128, 128), 0).astype(jnp.float32)

    def step(source, total):
        losses = arrived[source, 0:8, :]
        year = arrived[source, 8:16, :] - base
        upper = jnp.floor(year * (1.0 / 128.0))
        lower = year - 128.0 * upper
        spread = []
        for k in range(SUMM_DEV):
            first = jnp.broadcast_to(losses[:, k : k + 1], (8, 128))
            second = jnp.broadcast_to(losses[:, SUMM_DEV + k : SUMM_DEV + k + 1], (8, 128))
            spread.append(jnp.where(lane < 64, first, second))
        highs = [s.astype(jnp.bfloat16).astype(jnp.float32) for s in spread]
        lows = [s - h for s, h in zip(spread, highs)]
        for j in range(4):
            left, right = [], []
            for r in (2 * j, 2 * j + 1):
                match = upper_row == upper[r : r + 1]
                left.append(
                    jnp.concatenate([jnp.where(match, s[r : r + 1], 0.0) for s in highs + lows], axis=0).astype(
                        jnp.bfloat16
                    )
                )
                right.append((lower_row == lower[r : r + 1]).astype(jnp.bfloat16))
            total = total + lax.dot_general(
                jnp.concatenate(left, axis=1),
                jnp.concatenate(right, axis=1),
                NT,
                preferred_element_type=jnp.float32,
            )
        return total

    total = lax.fori_loop(0, arrived.shape[0], step, jnp.zeros((64, 128), jnp.float32))
    spare[...] = total[:32] + total[32:]
    for h in range(8):
        out[:, 128 * h : 128 * h + 128] = spare[pl.ds(h, SUMM_DEV, stride=8), :]


def per_device(
    ground_up,
    loc_deductible,
    loc_limit,
    block_policy,
    policy_deductible,
    policy_limit,
    policy_share,
    policy_summary,
    occurrence,
):
    owners = lax.axis_size("pol")
    shards = lax.axis_size("ev")
    compiler_params = pltpu.CompilerParams(vmem_limit_bytes=32 * 1024 * 1024)
    payload = pl.pallas_call(
        local_kernel,
        name="local",
        out_shape=jax.ShapeDtypeStruct((owners, 32, 128), jnp.float32),
        in_specs=[VMEM] * 8,
        out_specs=VMEM,
        scratch_shapes=[
            pltpu.VMEM((GROUP, 128, 256), jnp.bfloat16),
            pltpu.VMEM((8, 256), jnp.float32),
            pltpu.VMEM((8, 128), jnp.float32),
        ],
        compiler_params=compiler_params,
    )(
        ground_up,
        loc_deductible,
        loc_limit,
        block_policy[None],
        policy_deductible[None],
        policy_limit[None],
        policy_share[None],
        policy_summary[None],
    )
    arrived = lax.all_to_all(payload, "pol", split_axis=0, concat_axis=0, tiled=True)
    payload = pl.pallas_call(
        policy_kernel,
        name="policies",
        out_shape=jax.ShapeDtypeStruct((shards, 16, 128), jnp.float32),
        in_specs=[VMEM] * 2,
        out_specs=VMEM,
        scratch_shapes=[pltpu.VMEM((8, 128), jnp.float32)],
        compiler_params=compiler_params,
    )(arrived, occurrence)
    arrived = lax.all_to_all(payload, "ev", split_axis=0, concat_axis=0, tiled=True)
    return pl.pallas_call(
        year_kernel,
        name="years",
        out_shape=jax.ShapeDtypeStruct((SUMM_DEV, YR_DEV), jnp.float32),
        in_specs=[VMEM],
        out_specs=VMEM,
        scratch_shapes=[pltpu.VMEM((32, 128), jnp.float32)],
        compiler_params=compiler_params,
    )(arrived)


def solution(mesh):
    placed = (
        P("pol", "ev", None),
        P("pol", None),
        P("pol", None),
        P("pol"),
        P("pol"),
        P("pol"),
        P("pol"),
        P("pol"),
        P("ev", None),
    )
    return jax.shard_map(
        per_device, mesh=mesh, in_specs=placed, out_specs=P("pol", "ev"), check_vma=False
    )
```

```python
import jax
import jax.numpy as jnp
from jax import lax
from jax.experimental import pallas as pl
from jax.experimental.pallas import tpu as pltpu
from jax.sharding import PartitionSpec as P

SUMM_DEV = 4
YR_DEV = 1024
GROUP = 28
SLOT = 7
NT = (((1,), (1,)), ((), ()))
VMEM = pl.BlockSpec(memory_space=pltpu.VMEM)


def two_terms(x):
    high = x.astype(jnp.bfloat16)
    return high, (x - high.astype(jnp.float32)).astype(jnp.bfloat16)


def own_years_kernel(occurrence, out):
    turned = jnp.concatenate([occurrence[...].astype(jnp.float32).T, jnp.zeros((64, 112), jnp.float32)], axis=1)
    sub = lax.broadcasted_iota(jnp.int32, (64, 128), 0)
    turned = jnp.where(sub // 8 == lax.axis_index("pol"), turned, 0.0).reshape(8, 8, 128).sum(axis=0)
    moved = pltpu.roll(turned, 0, 1, stride=16, stride_axis=0)
    out[...] = jnp.broadcast_to(jnp.sum(moved, axis=0, keepdims=True), out.shape)


def local_kernel(ground, deduct, limit, owner, ded, lim, share, summ, out, terms, ids, params):
    blocks = ground.shape[0]
    terms[:, 16 * SLOT :, :] = jnp.zeros((GROUP, 128 - 16 * SLOT, 256), jnp.bfloat16)
    for i in range(SLOT):
        first = i * GROUP
        count = min(GROUP, blocks - first)
        lower = deduct[first : first + count].astype(jnp.float32)[:, None, :]
        upper = limit[first : first + count].astype(jnp.float32)[:, None, :]
        net = jnp.minimum(jnp.maximum(ground[first : first + count].astype(jnp.float32) - lower, 0.0), upper)
        high, low = two_terms(net)
        terms[:count, 16 * i : 16 * i + 16, :128] = high
        terms[:count, 16 * i : 16 * i + 16, 128:] = low
        if count < GROUP:
            terms[count:, 16 * i : 16 * i + 16, :] = jnp.zeros((GROUP - count, 16, 256), jnp.bfloat16)

    sub = lax.broadcasted_iota(jnp.int32, (8, 128), 0)
    lane = lax.broadcasted_iota(jnp.int32, (8, 128), 1)
    ids[...] = jnp.full((8, 256), -1.0, jnp.float32)
    ids[0:1, 0:blocks] = owner[...].astype(jnp.float32)
    flat = jnp.broadcast_to(ids[0:1, :], (8, 256))
    rows = jnp.full((8, 128), -1.0, jnp.float32)
    for i in range(SLOT):
        piece = flat if i == 0 else pltpu.roll(flat, 256 - i * GROUP, 1)
        rows = jnp.where(sub == i, piece[:, :128], rows)
    place = (lane == sub + 16 * SLOT).astype(jnp.float32)
    columns = lax.dot_general(
        rows, place, (((0,), (0,)), ((), ())), precision=lax.Precision.HIGHEST, preferred_element_type=jnp.float32
    )

    params[...] = jnp.zeros((8, 128), jnp.float32)
    params[4:5, 0:64] = ded[...]
    params[5:6, 0:64] = lim[...]
    params[6:7, 0:64] = share[...]
    params[7:8, 0:64] = summ[...].astype(jnp.float32)
    own = params[...]
    half = lax.rem(lax.axis_index("pol"), 2)
    own = jnp.where(lane // 64 == half, own + pltpu.roll(own, 64, 1), 0.0)

    ones = jnp.ones((8, 256), jnp.bfloat16)
    tiles = [jnp.zeros((8, 128), jnp.float32) for _ in range(4)]
    for n in range(GROUP // 2):
        weights = terms[2 * n : 2 * n + 2].reshape(256, 256)
        sums = lax.dot_general(ones, weights, NT, preferred_element_type=jnp.float32)
        for half_row in range(2):
            r = 2 * n + half_row
            tiles[r // 8] = jnp.where(sub == r % 8, sums[:, 128 * half_row : 128 * half_row + 128], tiles[r // 8])
    tiles = [tiles[t] + columns[8 * t : 8 * t + 8] for t in range(4)]
    tiles[3] = jnp.where(sub < 4, tiles[3], own)
    for t in range(4):
        out[8 * t : 8 * t + 8, :] = tiles[t]


def policy_kernel(arrived, out):
    owners = arrived.shape[0]
    policies = 64 * owners
    flat = arrived[:, :32, :].reshape(owners * 32, 128)
    turned = flat.T
    row = lax.broadcasted_iota(jnp.int32, (1, owners * 32), 1) % 32
    high, low = two_terms(turned[: 16 * SLOT])
    policy = lax.broadcasted_iota(jnp.int32, (policies, owners * 32), 0).astype(jnp.float32)
    total = jnp.zeros((32, policies), jnp.float32)
    for i in range(SLOT):
        ids = jnp.where(row < GROUP, turned[16 * SLOT + i : 16 * SLOT + i + 1], -1.0)
        member = (policy == ids).astype(jnp.bfloat16)
        left = jnp.concatenate([high[16 * i : 16 * i + 16], low[16 * i : 16 * i + 16]], axis=0)
        total = total + lax.dot_general(left, member, NT, preferred_element_type=jnp.float32)
    policy_ground = total[:16] + total[16:]

    pairs = [arrived[2 * k, 24:32, :] + arrived[2 * k + 1, 24:32, :] for k in range(owners // 2)]
    params = jnp.concatenate(pairs, axis=1)
    loss = params[6:7] * jnp.minimum(jnp.maximum(policy_ground - params[4:5], 0.0), params[5:6])
    own = lax.axis_index("pol") * SUMM_DEV
    group = lax.broadcasted_iota(jnp.int32, (8, policies), 0)
    wanted = jnp.where(group < SUMM_DEV, (group + own).astype(jnp.float32), -1.0)
    chosen = (wanted == params[7:8]).astype(jnp.float32)
    spread = jnp.concatenate([loss * chosen[SUMM_DEV - 1 - k : SUMM_DEV - k] for k in range(SUMM_DEV)], axis=0)
    high, low = two_terms(jnp.concatenate([spread, jnp.zeros((128 - 16 * SUMM_DEV, policies), jnp.float32)], axis=0))
    ones = jnp.ones((8, policies), jnp.bfloat16)
    sums = lax.dot_general(ones, high, NT, preferred_element_type=jnp.float32) + lax.dot_general(
        ones, low, NT, preferred_element_type=jnp.float32
    )
    place = lax.rem(lax.axis_index("ev"), 8)
    sums = pltpu.roll(sums, lax.rem(16 * (place + 8 - (SUMM_DEV - 1)), 128), 1)
    for k in range(out.shape[0] // 8):
        out[8 * k : 8 * k + 8, :] = sums


def count_kernel(arrived, out, uppers, lowers):
    eighths = arrived.shape[0]
    base = (lax.axis_index("ev") * YR_DEV).astype(jnp.float32)
    year = arrived[:, 32:64, :] - base
    upper = jnp.floor(year * (1.0 / 128.0))
    uppers[...] = upper
    lowers[...] = year - 128.0 * upper
    mine = lax.broadcasted_iota(jnp.int32, (16, 128), 1) % 16 == lax.broadcasted_iota(jnp.int32, (16, 128), 0)
    row = lax.broadcasted_iota(jnp.int32, (128, 128), 0).astype(jnp.float32).astype(jnp.bfloat16)
    one = jnp.ones((16, 128), jnp.bfloat16)
    zero = jnp.zeros((16, 128), jnp.bfloat16)

    def step(source, carry):
        total = jnp.zeros((128, 128), jnp.float32)
        for j in range(eighths // 2):
            left, right = [], []
            for p in (2 * j, 2 * j + 1):
                upper = jnp.broadcast_to(uppers[p, pl.ds(source, 1), :], (16, 128))
                upper = jnp.where(mine, upper, -1.0).astype(jnp.bfloat16)
                lower = jnp.broadcast_to(lowers[p, pl.ds(source, 1), :], (16, 128)).astype(jnp.bfloat16)
                left.append(
                    jnp.concatenate([jnp.where(upper == jnp.bfloat16(h), one, zero) for h in range(8)], axis=0)
                )
                right.append(
                    jnp.concatenate(
                        [jnp.where(row[16 * h : 16 * h + 16] == lower, one, zero) for h in range(8)], axis=0
                    )
                )
            total = total + lax.dot_general(
                jnp.concatenate(left, axis=1), jnp.concatenate(right, axis=1), NT, preferred_element_type=jnp.float32
            )
        total = total.astype(jnp.bfloat16)
        for h in range(8):
            out[pl.ds(pl.multiple_of(16 * source, 16), 16), 128 * h : 128 * h + 128] = total[16 * h : 16 * h + 16]
        return carry

    lax.fori_loop(0, arrived.shape[1] - 32, step, 0, unroll=4)


def year_kernel(arrived, counts, out):
    lane = lax.broadcasted_iota(jnp.int32, (8, 128), 1)
    sub = lax.broadcasted_iota(jnp.int32, (8, 128), 0)
    columns = []
    for group in range(arrived.shape[0] // 8):
        tile = jnp.zeros((8, 128), jnp.float32)
        for i in range(8):
            source = 8 * group + i
            row = jnp.broadcast_to(arrived[source : source + 1, :], (8, 128))
            tile = jnp.where((lane // 16 + sub) % 8 == i, row, tile)
        tile = pltpu.roll(tile, 0, 1, stride=16, stride_axis=0)
        columns.append(jnp.where(sub < SUMM_DEV, tile, 0.0))
    high, low = two_terms(jnp.concatenate(columns, axis=1))
    total = lax.dot_general(
        jnp.concatenate([high, low], axis=0), counts[...], (((1,), (0,)), ((), ())), preferred_element_type=jnp.float32
    )
    out[...] = total[0:SUMM_DEV] + total[8 : 8 + SUMM_DEV]


def per_device(
    ground_up,
    loc_deductible,
    loc_limit,
    block_policy,
    policy_deductible,
    policy_limit,
    policy_share,
    policy_summary,
    occurrence,
):
    owners = lax.axis_size("pol")
    shards = lax.axis_size("ev")
    compiler_params = pltpu.CompilerParams(vmem_limit_bytes=32 * 1024 * 1024)
    years = pl.pallas_call(
        own_years_kernel,
        name="own_years",
        out_shape=jax.ShapeDtypeStruct((shards, 128), jnp.float32),
        in_specs=[VMEM],
        out_specs=VMEM,
        compiler_params=compiler_params,
    )(occurrence)
    years = lax.all_to_all(years[:, None], "ev", split_axis=0, concat_axis=0, tiled=True)
    payload = pl.pallas_call(
        local_kernel,
        name="local",
        out_shape=jax.ShapeDtypeStruct((32, 128), jnp.float32),
        in_specs=[VMEM] * 8,
        out_specs=VMEM,
        scratch_shapes=[
            pltpu.VMEM((GROUP, 128, 256), jnp.bfloat16),
            pltpu.VMEM((8, 256), jnp.float32),
            pltpu.VMEM((8, 128), jnp.float32),
        ],
        compiler_params=compiler_params,
    )(
        ground_up,
        loc_deductible,
        loc_limit,
        block_policy[None],
        policy_deductible[None],
        policy_limit[None],
        policy_share[None],
        policy_summary[None],
    )
    payload = jnp.concatenate([payload, years[:, 0]], axis=0)
    payload = jnp.broadcast_to(payload[None], (owners, *payload.shape))
    arrived = lax.all_to_all(payload, "pol", split_axis=0, concat_axis=0, tiled=True)
    losses = pl.pallas_call(
        policy_kernel,
        name="policies",
        out_shape=jax.ShapeDtypeStruct((shards, 128), jnp.float32),
        in_specs=[VMEM],
        out_specs=VMEM,
        compiler_params=compiler_params,
    )(arrived)
    losses = lax.all_to_all(losses[:, None], "ev", split_axis=0, concat_axis=0, tiled=True)
    counts = pl.pallas_call(
        count_kernel,
        name="counts",
        out_shape=jax.ShapeDtypeStruct((16 * shards, YR_DEV), jnp.bfloat16),
        in_specs=[VMEM],
        out_specs=VMEM,
        scratch_shapes=[pltpu.VMEM((owners, shards, 128), jnp.float32)] * 2,
        compiler_params=compiler_params,
        cost_estimate=pl.CostEstimate(flops=1 << 32, bytes_accessed=1 << 20, transcendentals=0),
    )(arrived)
    return pl.pallas_call(
        year_kernel,
        name="years",
        out_shape=jax.ShapeDtypeStruct((SUMM_DEV, YR_DEV), jnp.float32),
        in_specs=[VMEM, VMEM],
        out_specs=VMEM,
        compiler_params=compiler_params,
    )(losses[:, 0], counts)


def solution(mesh):
    placed = (
        P("pol", "ev", None),
        P("pol", None),
        P("pol", None),
        P("pol"),
        P("pol"),
        P("pol"),
        P("pol"),
        P("pol"),
        P("ev", None),
    )
    return jax.shard_map(
        per_device, mesh=mesh, in_specs=placed, out_specs=P("pol", "ev"), check_vma=False
    )
```

```python
import jax
import jax.numpy as jnp
from jax import lax
from jax.experimental import pallas as pl
from jax.experimental.pallas import tpu as pltpu
from jax.sharding import PartitionSpec as P

SUMM_DEV = 4
YR_DEV = 1024
GROUP = 28
SLOT = 7
NT = (((1,), (1,)), ((), ()))
VMEM = pl.BlockSpec(memory_space=pltpu.VMEM)


def two_terms(x):
    high = x.astype(jnp.bfloat16)
    return high, (x - high.astype(jnp.float32)).astype(jnp.bfloat16)


def local_kernel(ground, deduct, limit, owner, ded, lim, share, summ, out, terms, ids, params):
    blocks = ground.shape[0]
    terms[:, 16 * SLOT :, :] = jnp.zeros((GROUP, 128 - 16 * SLOT, 256), jnp.bfloat16)
    for i in range(SLOT):
        first = i * GROUP
        count = min(GROUP, blocks - first)
        lower = deduct[first : first + count].astype(jnp.float32)[:, None, :]
        upper = limit[first : first + count].astype(jnp.float32)[:, None, :]
        net = jnp.minimum(jnp.maximum(ground[first : first + count].astype(jnp.float32) - lower, 0.0), upper)
        high, low = two_terms(net)
        terms[:count, 16 * i : 16 * i + 16, :128] = high
        terms[:count, 16 * i : 16 * i + 16, 128:] = low
        if count < GROUP:
            terms[count:, 16 * i : 16 * i + 16, :] = jnp.zeros((GROUP - count, 16, 256), jnp.bfloat16)

    sub = lax.broadcasted_iota(jnp.int32, (8, 128), 0)
    lane = lax.broadcasted_iota(jnp.int32, (8, 128), 1)
    ids[...] = jnp.full((8, 256), -1.0, jnp.float32)
    ids[0:1, 0:blocks] = owner[...].astype(jnp.float32)
    flat = jnp.broadcast_to(ids[0:1, :], (8, 256))
    rows = jnp.full((8, 128), -1.0, jnp.float32)
    for i in range(SLOT):
        piece = flat if i == 0 else pltpu.roll(flat, 256 - i * GROUP, 1)
        rows = jnp.where(sub == i, piece[:, :128], rows)
    place = (lane == sub + 16 * SLOT).astype(jnp.float32)
    columns = lax.dot_general(
        rows, place, (((0,), (0,)), ((), ())), precision=lax.Precision.HIGHEST, preferred_element_type=jnp.float32
    )

    params[...] = jnp.zeros((8, 128), jnp.float32)
    params[4:5, 0:64] = ded[...]
    params[5:6, 0:64] = lim[...]
    params[6:7, 0:64] = share[...]
    params[7:8, 0:64] = summ[...].astype(jnp.float32)
    own = params[...]
    half = lax.rem(lax.axis_index("pol"), 2)
    own = jnp.where(lane // 64 == half, own + pltpu.roll(own, 64, 1), 0.0)

    ones = jnp.ones((8, 256), jnp.bfloat16)
    tiles = [jnp.zeros((8, 128), jnp.float32) for _ in range(4)]
    for n in range(GROUP // 2):
        weights = terms[2 * n : 2 * n + 2].reshape(256, 256)
        sums = lax.dot_general(ones, weights, NT, preferred_element_type=jnp.float32)
        for half_row in range(2):
            r = 2 * n + half_row
            tiles[r // 8] = jnp.where(sub == r % 8, sums[:, 128 * half_row : 128 * half_row + 128], tiles[r // 8])
    tiles = [tiles[t] + columns[8 * t : 8 * t + 8] for t in range(4)]
    tiles[3] = jnp.where(sub < 4, tiles[3], own)
    for t in range(4):
        for k in range(out.shape[0]):
            out[k, 8 * t : 8 * t + 8, :] = tiles[t]


def policy_kernel(arrived, occurrence, out):
    owners = arrived.shape[0]
    policies = 64 * owners
    flat = arrived[...].reshape(owners * 32, 128)
    turned = flat.T
    row = lax.broadcasted_iota(jnp.int32, (1, owners * 32), 1) % 32
    high, low = two_terms(turned[: 16 * SLOT])
    policy = lax.broadcasted_iota(jnp.int32, (policies, owners * 32), 0).astype(jnp.float32)
    total = jnp.zeros((32, policies), jnp.float32)
    for i in range(SLOT):
        ids = jnp.where(row < GROUP, turned[16 * SLOT + i : 16 * SLOT + i + 1], -1.0)
        member = (policy == ids).astype(jnp.bfloat16)
        left = jnp.concatenate([high[16 * i : 16 * i + 16], low[16 * i : 16 * i + 16]], axis=0)
        total = total + lax.dot_general(left, member, NT, preferred_element_type=jnp.float32)
    policy_ground = total[:16] + total[16:]

    pairs = [arrived[2 * k, 24:32, :] + arrived[2 * k + 1, 24:32, :] for k in range(owners // 2)]
    params = jnp.concatenate(pairs, axis=1)
    loss = params[6:7] * jnp.minimum(jnp.maximum(policy_ground - params[4:5], 0.0), params[5:6])
    own = lax.axis_index("pol") * SUMM_DEV
    group = lax.broadcasted_iota(jnp.int32, (8, policies), 0)
    wanted = jnp.where(group < SUMM_DEV, (group + own).astype(jnp.float32), -1.0)
    chosen = (wanted == params[7:8]).astype(jnp.float32)
    spread = jnp.concatenate([loss * chosen[k : k + 1] for k in range(SUMM_DEV)], axis=0)
    high, low = two_terms(jnp.concatenate([spread, jnp.zeros((128 - 16 * SUMM_DEV, policies), jnp.float32)], axis=0))
    ones = jnp.ones((8, policies), jnp.bfloat16)
    sums = lax.dot_general(ones, high, NT, preferred_element_type=jnp.float32) + lax.dot_general(
        ones, low, NT, preferred_element_type=jnp.float32
    )
    turned = jnp.concatenate([occurrence[...].astype(jnp.float32).T, jnp.zeros((64, 112), jnp.float32)], axis=1)
    tiles = [turned[8 * r : 8 * r + 8] for r in range(8)]
    tiles = [pltpu.roll(t, 0, 1, stride=16, stride_axis=0) for t in tiles]
    rows = [sums[0:1]] + [jnp.sum(t, axis=0, keepdims=True) for t in tiles]
    nine = jnp.concatenate(rows, axis=0)
    for k in range(out.shape[0] // 9):
        out[9 * k : 9 * k + 9, :] = nine


def year_kernel(arrived, out, uppers, lowers, spread, spare):
    sources = arrived.shape[0] // 9
    base = (lax.axis_index("ev") * YR_DEV).astype(jnp.float32)
    year = arrived[...] - base
    upper = jnp.floor(year * (1.0 / 128.0))
    uppers[...] = upper
    lowers[...] = year - 128.0 * upper

    high, low = two_terms(arrived[pl.ds(0, sources, stride=9), :])
    lane = lax.broadcasted_iota(jnp.int32, (128, 128), 1)
    sub = lax.broadcasted_iota(jnp.int32, (128, 128), 0)
    repeat = jnp.concatenate(
        [(sub == lane % 16 + 16 * k).astype(jnp.float32).astype(jnp.bfloat16) for k in range(SUMM_DEV)], axis=1
    )
    spread[...] = jnp.dot(jnp.concatenate([high, low], axis=0), repeat, preferred_element_type=jnp.float32)

    row = sub.astype(jnp.float32).astype(jnp.bfloat16)
    upper_row = (lax.broadcasted_iota(jnp.int32, (16, 128), 0) % 8).astype(jnp.float32).astype(jnp.bfloat16)
    one = jnp.ones((16, 128), jnp.bfloat16)
    zero = jnp.zeros((16, 128), jnp.bfloat16)

    def step(source, total):
        losses = []
        for term in range(2):
            values = spread[pl.ds(term * sources + source, 1), :]
            for k in range(0, SUMM_DEV, 2):
                pair = [jnp.broadcast_to(values[:, 128 * (k + i) : 128 * (k + i) + 128], (8, 128)) for i in range(2)]
                losses.append(jnp.concatenate(pair, axis=0).astype(jnp.bfloat16))
        left, right = [], []
        for r in range(8):
            at = pl.ds(9 * source + 1 + r, 1)
            upper = jnp.broadcast_to(uppers[at, :], (16, 128)).astype(jnp.bfloat16)
            lower = jnp.broadcast_to(lowers[at, :], (16, 128)).astype(jnp.bfloat16)
            match = upper == upper_row
            left.append(jnp.concatenate([jnp.where(match, x, zero) for x in losses], axis=0))
            right.append(
                jnp.concatenate([jnp.where(row[16 * h : 16 * h + 16] == lower, one, zero) for h in range(8)], axis=0)
            )
        return total + lax.dot_general(
            jnp.concatenate(left, axis=1), jnp.concatenate(right, axis=1), NT, preferred_element_type=jnp.float32
        )

    total = lax.fori_loop(0, sources, step, jnp.zeros((64, 128), jnp.float32), unroll=4)
    spare[...] = total[:32] + total[32:]
    for h in range(8):
        out[:, 128 * h : 128 * h + 128] = spare[pl.ds(h, SUMM_DEV, stride=8), :]


def per_device(
    ground_up,
    loc_deductible,
    loc_limit,
    block_policy,
    policy_deductible,
    policy_limit,
    policy_share,
    policy_summary,
    occurrence,
):
    owners = lax.axis_size("pol")
    shards = lax.axis_size("ev")
    compiler_params = pltpu.CompilerParams(vmem_limit_bytes=32 * 1024 * 1024)
    payload = pl.pallas_call(
        local_kernel,
        name="local",
        out_shape=jax.ShapeDtypeStruct((owners, 32, 128), jnp.float32),
        in_specs=[VMEM] * 8,
        out_specs=VMEM,
        scratch_shapes=[
            pltpu.VMEM((GROUP, 128, 256), jnp.bfloat16),
            pltpu.VMEM((8, 256), jnp.float32),
            pltpu.VMEM((8, 128), jnp.float32),
        ],
        compiler_params=compiler_params,
    )(
        ground_up,
        loc_deductible,
        loc_limit,
        block_policy[None],
        policy_deductible[None],
        policy_limit[None],
        policy_share[None],
        policy_summary[None],
    )
    arrived = lax.all_to_all(payload, "pol", split_axis=0, concat_axis=0, tiled=True)
    payload = pl.pallas_call(
        policy_kernel,
        name="policies",
        out_shape=jax.ShapeDtypeStruct((9 * shards, 128), jnp.float32),
        in_specs=[VMEM] * 2,
        out_specs=VMEM,
        compiler_params=compiler_params,
    )(arrived, occurrence)
    arrived = lax.all_to_all(payload[:, None], "ev", split_axis=0, concat_axis=0, tiled=True)
    return pl.pallas_call(
        year_kernel,
        name="years",
        out_shape=jax.ShapeDtypeStruct((SUMM_DEV, YR_DEV), jnp.float32),
        in_specs=[VMEM],
        out_specs=VMEM,
        scratch_shapes=[
            pltpu.VMEM((9 * shards, 128), jnp.float32),
            pltpu.VMEM((9 * shards, 128), jnp.float32),
            pltpu.VMEM((2 * shards, 128 * SUMM_DEV), jnp.float32),
            pltpu.VMEM((32, 128), jnp.float32),
        ],
        compiler_params=compiler_params,
    )(arrived[:, 0])


def solution(mesh):
    placed = (
        P("pol", "ev", None),
        P("pol", None),
        P("pol", None),
        P("pol"),
        P("pol"),
        P("pol"),
        P("pol"),
        P("pol"),
        P("ev", None),
    )
    return jax.shard_map(
        per_device, mesh=mesh, in_specs=placed, out_specs=P("pol", "ev"), check_vma=False
    )
```

```python
import jax
import jax.numpy as jnp
from jax import lax
from jax.experimental import pallas as pl
from jax.experimental.pallas import tpu as pltpu
from jax.sharding import PartitionSpec as P

SUMM_DEV = 4
YR_DEV = 1024
GROUP = 28
SLOT = 7
NT = (((1,), (1,)), ((), ()))
VMEM = pl.BlockSpec(memory_space=pltpu.VMEM)


def two_terms(x):
    high = x.astype(jnp.bfloat16)
    return high, (x - high.astype(jnp.float32)).astype(jnp.bfloat16)


def local_kernel(
    ground_hbm,
    deduct_hbm,
    limit_hbm,
    owner_hbm,
    ded_hbm,
    lim_hbm,
    share_hbm,
    summ_hbm,
    out,
    ground,
    deduct,
    limit,
    owner,
    ded,
    lim,
    share,
    summ,
    terms,
    ids,
    params,
    sems,
):
    blocks = ground.shape[0]
    part = 4 * SLOT
    bounds = [(first, min(part, blocks - first)) for first in range(0, GROUP * SLOT, part)]
    small = [
        (owner_hbm, owner),
        (ded_hbm, ded),
        (lim_hbm, lim),
        (share_hbm, share),
        (summ_hbm, summ),
    ]
    pairs = small + [(deduct_hbm, deduct), (limit_hbm, limit)]
    pairs += [(ground_hbm.at[first : first + count], ground.at[first : first + count]) for first, count in bounds]
    copies = [pltpu.make_async_copy(source, target, sems.at[n]) for n, (source, target) in enumerate(pairs)]
    for copy in copies:
        copy.start()
    sub = lax.broadcasted_iota(jnp.int32, (8, 128), 0)
    lane = lax.broadcasted_iota(jnp.int32, (8, 128), 1)
    terms[:, 16 * SLOT :, :] = jnp.zeros((GROUP, 128 - 16 * SLOT, 256), jnp.bfloat16)
    ids[...] = jnp.full((8, 256), -1.0, jnp.float32)
    params[...] = jnp.zeros((8, 128), jnp.float32)
    for copy in copies:
        copy.wait()

    ids[0:1, 0:blocks] = owner[...].astype(jnp.float32)
    block = lax.broadcasted_iota(jnp.int32, (32, 256), 1).astype(jnp.float32)
    at_row = jnp.floor((block + 0.5) * (1.0 / SLOT)) == lax.broadcasted_iota(jnp.int32, (32, 256), 0).astype(jnp.float32)
    policy = ids[0:1, :]
    upper = 256.0 * jnp.floor(policy * (1.0 / 256.0))
    left = jnp.concatenate([jnp.where(at_row, upper, 0.0), jnp.where(at_row, policy - upper, 0.0)], axis=0)
    block = lax.broadcasted_iota(jnp.int32, (256, 128), 0).astype(jnp.float32)
    block = block - SLOT * jnp.floor((block + 0.5) * (1.0 / SLOT))
    right = block + 16.0 * SLOT == lax.broadcasted_iota(jnp.int32, (256, 128), 1).astype(jnp.float32)
    columns = jnp.dot(
        left.astype(jnp.bfloat16), right.astype(jnp.float32).astype(jnp.bfloat16), preferred_element_type=jnp.float32
    )
    columns = columns[:32] + columns[32:]
    params[4:5, 0:64] = ded[...]
    params[5:6, 0:64] = lim[...]
    params[6:7, 0:64] = share[...]
    params[7:8, 0:64] = summ[...].astype(jnp.float32)
    own = params[...]
    half = lax.rem(lax.axis_index("pol"), 2)
    own = jnp.where(lane // 64 == half, own + pltpu.roll(own, 64, 1), 0.0)

    ones = jnp.ones((8, 256), jnp.bfloat16)
    tiles = [jnp.zeros((8, 128), jnp.float32) for _ in range(4)]
    for c, (first, count) in enumerate(bounds):
        lower = deduct[first : first + count].astype(jnp.float32)[:, None, :]
        upper = limit[first : first + count].astype(jnp.float32)[:, None, :]
        net = jnp.minimum(jnp.maximum(ground[first : first + count].astype(jnp.float32) - lower, 0.0), upper)
        for term, value in enumerate(two_terms(net)):
            at = slice(128 * term, 128 * term + 128)
            whole = count // SLOT
            terms[4 * c : 4 * c + whole, : 16 * SLOT, at] = value[: whole * SLOT].reshape(whole, 16 * SLOT, 128)
            rest = count - whole * SLOT
            if rest:
                terms[4 * c + whole, : 16 * rest, at] = value[whole * SLOT :].reshape(16 * rest, 128)
                terms[4 * c + whole, 16 * rest : 16 * SLOT, at] = jnp.zeros((16 * (SLOT - rest), 128), jnp.bfloat16)
        for n in (2 * c, 2 * c + 1):
            weights = terms[2 * n : 2 * n + 2].reshape(256, 256)
            sums = lax.dot_general(ones, weights, NT, preferred_element_type=jnp.float32)
            for half_row in range(2):
                r = 2 * n + half_row
                tiles[r // 8] = jnp.where(sub == r % 8, sums[:, 128 * half_row : 128 * half_row + 128], tiles[r // 8])
    tiles = [tiles[t] + columns[8 * t : 8 * t + 8] for t in range(4)]
    tiles[3] = jnp.where(sub < 4, tiles[3], own)
    for t in range(4):
        for k in range(out.shape[0]):
            out[k, 8 * t : 8 * t + 8, :] = tiles[t]


def policy_kernel(arrived, occurrence, out):
    owners = arrived.shape[0]
    policies = 64 * owners
    flat = arrived[...].reshape(owners * 32, 128)
    turned = flat.T
    row = lax.broadcasted_iota(jnp.int32, (1, owners * 32), 1) % 32
    high, low = two_terms(turned[: 16 * SLOT])
    policy = lax.broadcasted_iota(jnp.int32, (policies, owners * 32), 0).astype(jnp.float32)
    total = jnp.zeros((32, policies), jnp.float32)
    for i in range(SLOT):
        ids = jnp.where(row < GROUP, turned[16 * SLOT + i : 16 * SLOT + i + 1], -1.0)
        member = (policy == ids).astype(jnp.bfloat16)
        left = jnp.concatenate([high[16 * i : 16 * i + 16], low[16 * i : 16 * i + 16]], axis=0)
        total = total + lax.dot_general(left, member, NT, preferred_element_type=jnp.float32)
    policy_ground = total[:16] + total[16:]

    pairs = [arrived[2 * k, 24:32, :] + arrived[2 * k + 1, 24:32, :] for k in range(owners // 2)]
    params = jnp.concatenate(pairs, axis=1)
    loss = params[6:7] * jnp.minimum(jnp.maximum(policy_ground - params[4:5], 0.0), params[5:6])
    own = lax.axis_index("pol") * SUMM_DEV
    group = lax.broadcasted_iota(jnp.int32, (8, policies), 0)
    wanted = jnp.where(group < SUMM_DEV, (group + own).astype(jnp.float32), -1.0)
    chosen = (wanted == params[7:8]).astype(jnp.float32)
    spread = jnp.concatenate([loss * chosen[k : k + 1] for k in range(SUMM_DEV)], axis=0)
    high, low = two_terms(jnp.concatenate([spread, jnp.zeros((128 - 16 * SUMM_DEV, policies), jnp.float32)], axis=0))
    ones = jnp.ones((8, policies), jnp.bfloat16)
    sums = lax.dot_general(ones, high, NT, preferred_element_type=jnp.float32) + lax.dot_general(
        ones, low, NT, preferred_element_type=jnp.float32
    )
    turned = jnp.concatenate([occurrence[...].astype(jnp.float32).T, jnp.zeros((64, 112), jnp.float32)], axis=1)
    tiles = [turned[8 * r : 8 * r + 8] for r in range(8)]
    tiles = [pltpu.roll(t, 0, 1, stride=16, stride_axis=0) for t in tiles]
    rows = [sums[0:1]] + [jnp.sum(t, axis=0, keepdims=True) for t in tiles]
    nine = jnp.concatenate(rows, axis=0)
    for k in range(out.shape[0] // 9):
        out[9 * k : 9 * k + 9, :] = nine


def year_kernel(arrived, out, uppers, lowers, spread, spare):
    sources = arrived.shape[0] // 9
    base = (lax.axis_index("ev") * YR_DEV).astype(jnp.float32)
    year = arrived[...] - base
    upper = jnp.floor(year * (1.0 / 128.0))
    uppers[...] = upper
    lowers[...] = year - 128.0 * upper

    high, low = two_terms(arrived[pl.ds(0, sources, stride=9), :])
    lane = lax.broadcasted_iota(jnp.int32, (128, 128), 1)
    sub = lax.broadcasted_iota(jnp.int32, (128, 128), 0)
    repeat = jnp.concatenate(
        [(sub == lane % 16 + 16 * k).astype(jnp.float32).astype(jnp.bfloat16) for k in range(SUMM_DEV)], axis=1
    )
    spread[...] = jnp.dot(jnp.concatenate([high, low], axis=0), repeat, preferred_element_type=jnp.float32)

    row = sub.astype(jnp.float32).astype(jnp.bfloat16)
    upper_row = (lax.broadcasted_iota(jnp.int32, (16, 128), 0) % 8).astype(jnp.float32).astype(jnp.bfloat16)
    one = jnp.ones((16, 128), jnp.bfloat16)
    zero = jnp.zeros((16, 128), jnp.bfloat16)

    def step(source, total):
        losses = []
        for term in range(2):
            values = spread[pl.ds(term * sources + source, 1), :]
            for k in range(0, SUMM_DEV, 2):
                pair = [jnp.broadcast_to(values[:, 128 * (k + i) : 128 * (k + i) + 128], (8, 128)) for i in range(2)]
                losses.append(jnp.concatenate(pair, axis=0).astype(jnp.bfloat16))
        left, right = [], []
        for r in range(1, 9):
            at = pl.ds(9 * source + r, 1)
            upper = jnp.broadcast_to(uppers[at, :], (16, 128)).astype(jnp.bfloat16)
            lower = jnp.broadcast_to(lowers[at, :], (16, 128)).astype(jnp.bfloat16)
            match = upper == upper_row
            right.append(jnp.concatenate([jnp.where(match, x, zero) for x in losses], axis=0))
            left.append(
                jnp.concatenate([jnp.where(row[16 * h : 16 * h + 16] == lower, one, zero) for h in range(8)], axis=0)
            )
        return total + lax.dot_general(
            jnp.concatenate(left, axis=1), jnp.concatenate(right, axis=1), NT, preferred_element_type=jnp.float32
        )

    total = lax.fori_loop(0, sources, step, jnp.zeros((128, 64), jnp.float32), unroll=8).T
    spare[...] = total[:32] + total[32:]
    for h in range(8):
        out[:, 128 * h : 128 * h + 128] = spare[pl.ds(h, SUMM_DEV, stride=8), :]


def per_device(
    ground_up,
    loc_deductible,
    loc_limit,
    block_policy,
    policy_deductible,
    policy_limit,
    policy_share,
    policy_summary,
    occurrence,
):
    owners = lax.axis_size("pol")
    shards = lax.axis_size("ev")
    compiler_params = pltpu.CompilerParams(vmem_limit_bytes=32 * 1024 * 1024)
    payload = pl.pallas_call(
        local_kernel,
        name="local",
        out_shape=jax.ShapeDtypeStruct((owners, 32, 128), jnp.float32),
        in_specs=[pl.BlockSpec(memory_space=pltpu.HBM)] * 8,
        out_specs=VMEM,
        scratch_shapes=[
            pltpu.VMEM(ground_up.shape, jnp.bfloat16),
            pltpu.VMEM(loc_deductible.shape, jnp.bfloat16),
            pltpu.VMEM(loc_limit.shape, jnp.bfloat16),
            pltpu.VMEM((1, block_policy.shape[0]), jnp.int32),
            pltpu.VMEM((1, 64), jnp.float32),
            pltpu.VMEM((1, 64), jnp.float32),
            pltpu.VMEM((1, 64), jnp.float32),
            pltpu.VMEM((1, 64), jnp.int32),
            pltpu.VMEM((GROUP, 128, 256), jnp.bfloat16),
            pltpu.VMEM((8, 256), jnp.float32),
            pltpu.VMEM((8, 128), jnp.float32),
            pltpu.SemaphoreType.DMA((2 + SLOT + 5,)),
        ],
        compiler_params=compiler_params,
    )(
        pltpu.with_memory_space_constraint(ground_up, pltpu.HBM),
        pltpu.with_memory_space_constraint(loc_deductible, pltpu.HBM),
        pltpu.with_memory_space_constraint(loc_limit, pltpu.HBM),
        pltpu.with_memory_space_constraint(block_policy[None], pltpu.HBM),
        pltpu.with_memory_space_constraint(policy_deductible[None], pltpu.HBM),
        pltpu.with_memory_space_constraint(policy_limit[None], pltpu.HBM),
        pltpu.with_memory_space_constraint(policy_share[None], pltpu.HBM),
        pltpu.with_memory_space_constraint(policy_summary[None], pltpu.HBM),
    )
    arrived = lax.all_to_all(payload, "pol", split_axis=0, concat_axis=0, tiled=True)
    payload = pl.pallas_call(
        policy_kernel,
        name="policies",
        out_shape=jax.ShapeDtypeStruct((9 * shards, 128), jnp.float32),
        in_specs=[VMEM] * 2,
        out_specs=VMEM,
        compiler_params=compiler_params,
    )(arrived, occurrence)
    payload = payload.reshape(shards, 1, 9 * 128)
    arrived = lax.all_to_all(payload, "ev", split_axis=0, concat_axis=0, tiled=True)
    return pl.pallas_call(
        year_kernel,
        name="years",
        out_shape=jax.ShapeDtypeStruct((SUMM_DEV, YR_DEV), jnp.float32),
        in_specs=[VMEM],
        out_specs=VMEM,
        scratch_shapes=[
            pltpu.VMEM((9 * shards, 128), jnp.float32),
            pltpu.VMEM((9 * shards, 128), jnp.float32),
            pltpu.VMEM((2 * shards, 128 * SUMM_DEV), jnp.float32),
            pltpu.VMEM((32, 128), jnp.float32),
        ],
        compiler_params=compiler_params,
    )(arrived.reshape(9 * shards, 128))


def solution(mesh):
    placed = (
        P("pol", "ev", None),
        P("pol", None),
        P("pol", None),
        P("pol"),
        P("pol"),
        P("pol"),
        P("pol"),
        P("pol"),
        P("ev", None),
    )
    return jax.shard_map(
        per_device, mesh=mesh, in_specs=placed, out_specs=P("pol", "ev"), check_vma=False
    )
```

```python
import functools

import jax
import jax.numpy as jnp
from jax import lax
from jax.experimental import pallas as pl
from jax.experimental.pallas import tpu as pltpu
from jax.sharding import PartitionSpec as P

SUMM_DEV = 4
YR_DEV = 1024
GROUP = 28
SLOT = 7
SLOTS = 16
NT = (((1,), (1,)), ((), ()))
VMEM = pl.BlockSpec(memory_space=pltpu.VMEM)


def two_terms(x):
    high = x.astype(jnp.bfloat16)
    return high, (x - high.astype(jnp.float32)).astype(jnp.bfloat16)


def local_kernel(
    ground_hbm,
    deduct_hbm,
    limit_hbm,
    owner_hbm,
    ded_hbm,
    lim_hbm,
    share_hbm,
    summ_hbm,
    years_hbm,
    out,
    out_years,
    ground,
    deduct,
    limit,
    owner,
    ded,
    lim,
    share,
    summ,
    years,
    terms,
    ids,
    params,
    sems,
):
    blocks = ground.shape[0]
    part = 4 * SLOT
    bounds = [(first, min(part, blocks - first)) for first in range(0, GROUP * SLOT, part)]
    small = [
        (years_hbm, years),
        (owner_hbm, owner),
        (ded_hbm, ded),
        (lim_hbm, lim),
        (share_hbm, share),
        (summ_hbm, summ),
    ]
    pairs = small + [(deduct_hbm, deduct), (limit_hbm, limit)]
    pairs += [(ground_hbm.at[first : first + count], ground.at[first : first + count]) for first, count in bounds]
    copies = [pltpu.make_async_copy(source, target, sems.at[n]) for n, (source, target) in enumerate(pairs)]
    for copy in copies:
        copy.start()
    sub = lax.broadcasted_iota(jnp.int32, (8, 128), 0)
    lane = lax.broadcasted_iota(jnp.int32, (8, 128), 1)
    terms[:, 16 * SLOT :, :] = jnp.zeros((GROUP // 2, 128 - 16 * SLOT, 256), jnp.bfloat16)
    ids[...] = jnp.full((8, 256), -1.0, jnp.float32)
    params[...] = jnp.zeros((8, 128), jnp.float32)
    for copy in copies[: len(small)]:
        copy.wait()

    half_members, key, code, over = rank_years(years)
    ids[0:1, 0:blocks] = owner[...].astype(jnp.float32)
    block = lax.broadcasted_iota(jnp.int32, (32, 256), 1).astype(jnp.float32)
    at_row = jnp.floor((block + 0.5) * (1.0 / SLOT)) == lax.broadcasted_iota(jnp.int32, (32, 256), 0).astype(jnp.float32)
    policy = ids[0:1, :]
    upper = 256.0 * jnp.floor(policy * (1.0 / 256.0))
    left = jnp.concatenate([jnp.where(at_row, upper, 0.0), jnp.where(at_row, policy - upper, 0.0)], axis=0)
    block = lax.broadcasted_iota(jnp.int32, (256, 128), 0).astype(jnp.float32)
    block = block - SLOT * jnp.floor((block + 0.5) * (1.0 / SLOT))
    right = block + 16.0 * SLOT == lax.broadcasted_iota(jnp.int32, (256, 128), 1).astype(jnp.float32)
    columns = jnp.dot(
        left.astype(jnp.bfloat16), right.astype(jnp.float32).astype(jnp.bfloat16), preferred_element_type=jnp.float32
    )
    columns = columns[:32] + columns[32:]
    params[4:5, 0:64] = ded[...]
    params[5:6, 0:64] = lim[...]
    params[6:7, 0:64] = share[...]
    params[7:8, 0:64] = summ[...].astype(jnp.float32)
    own = params[...]
    half = lax.rem(lax.axis_index("pol"), 2)
    own = jnp.where(lane // 64 == half, own + pltpu.roll(own, 64, 1), 0.0)

    for copy in copies[len(small) :]:
        copy.wait()
    out_years[...] = place_years(half_members, key, code, over)
    parity = lax.broadcasted_iota(jnp.int32, (8, 256), 0) % 2
    side = (lax.broadcasted_iota(jnp.int32, (8, 256), 1) // 64) % 2
    ones = (parity == side).astype(jnp.float32).astype(jnp.bfloat16)
    low_lanes = lax.broadcasted_iota(jnp.int32, (1, SLOT, 16, 128), 3) < 64
    tiles = [jnp.zeros((8, 128), jnp.float32) for _ in range(4)]
    for c, (first, count) in enumerate(bounds):
        lower = deduct[first : first + count].astype(jnp.float32)[:, None, :]
        upper = limit[first : first + count].astype(jnp.float32)[:, None, :]
        net = jnp.minimum(jnp.maximum(ground[first : first + count].astype(jnp.float32) - lower, 0.0), upper)
        net = net + pltpu.roll(net.reshape(16 * count, 128), 64, 1).reshape(net.shape)
        if count < part:
            net = jnp.concatenate([net, jnp.zeros((part - count, 16, 128), jnp.float32)], axis=0)
        net = net.reshape(2, 2, SLOT, 16, 128)
        both = jnp.where(low_lanes, net[:, 0], net[:, 1])
        for term, value in enumerate(two_terms(both)):
            terms[2 * c : 2 * c + 2, : 16 * SLOT, 128 * term : 128 * term + 128] = value.reshape(2, 16 * SLOT, 128)
        weights = terms[2 * c : 2 * c + 2].reshape(256, 256)
        sums = lax.dot_general(ones, weights, NT, preferred_element_type=jnp.float32)
        for n in (2 * c, 2 * c + 1):
            piece = sums[:, 128 * (n % 2) : 128 * (n % 2) + 128]
            tiles[n // 4] = jnp.where(sub // 2 == n % 4, piece, tiles[n // 4])
    tiles = [tiles[t] + columns[8 * t : 8 * t + 8] for t in range(4)]
    tiles[3] = jnp.where(sub < 4, tiles[3], own)
    for t in range(4):
        for k in range(out.shape[0]):
            out[k, 8 * t : 8 * t + 8, :] = tiles[t]


def rank_years(years):
    shards = 32
    year = jnp.concatenate([years[pl.ds(0, 8, stride=2), :], years[pl.ds(1, 8, stride=2), :]], axis=1).astype(jnp.float32)
    shard = jnp.floor(year * (1.0 / YR_DEV))
    code = year - YR_DEV * shard + 1.0
    shard_row = lax.broadcasted_iota(jnp.int32, (shards, 128), 0).astype(jnp.float32)
    member = [(shard_row == shard[r : r + 1]).astype(jnp.float32) for r in range(8)]
    half = [jnp.concatenate([member[2 * j], member[2 * j + 1]], axis=1) for j in range(4)]
    first = lax.broadcasted_iota(jnp.int32, (256, 256), 0)
    second = lax.broadcasted_iota(jnp.int32, (256, 256), 1)
    before = ((first // 64 == second // 64) & (first < second)).astype(jnp.float32).astype(jnp.bfloat16)
    stacked = jnp.concatenate(half, axis=0)
    ahead = jnp.dot(stacked.astype(jnp.bfloat16), before, preferred_element_type=jnp.float32)
    rank = jnp.sum((stacked * ahead).reshape(4, shards, 256), axis=1)
    event = lax.broadcasted_iota(jnp.int32, (4, 256), 1) // 64 + 4 * lax.broadcasted_iota(jnp.int32, (4, 256), 0)
    key = 16.0 * rank + event.astype(jnp.float32)
    most = jnp.max(jnp.max(rank, axis=0, keepdims=True), axis=1, keepdims=True)
    return jnp.concatenate(half, axis=1).astype(jnp.bfloat16), key, code, jnp.where(most >= SLOTS, -1.0, 0.0)


def place_years(members, key, code, over):
    slot_row = lax.broadcasted_iota(jnp.int32, (16 * SLOTS, 256), 0).astype(jnp.float32)
    upper = jnp.floor(code * (1.0 / 16.0))
    sums = []
    for value in (upper, code - 16.0 * upper):
        right = []
        for j in range(4):
            flat = jnp.concatenate([value[2 * j : 2 * j + 1], value[2 * j + 1 : 2 * j + 2]], axis=1)
            right.append(jnp.where(slot_row == key[j : j + 1], flat, 0.0).astype(jnp.bfloat16))
        sums.append(lax.dot_general(members, jnp.concatenate(right, axis=1), NT, preferred_element_type=jnp.float32))
    return jnp.concatenate([16.0 * sums[0] + sums[1], jnp.broadcast_to(over, (8, 16 * SLOTS))], axis=0)


def policy_kernel(arrived, compact, out):
    owners = arrived.shape[0]
    policies = 64 * owners
    flat = arrived[...].reshape(owners * 32, 128)
    turned = flat.T
    row = lax.broadcasted_iota(jnp.int32, (1, owners * 32), 1) % 32
    high, low = two_terms(turned[: 16 * SLOT])
    policy = lax.broadcasted_iota(jnp.int32, (policies, owners * 32), 0).astype(jnp.float32)
    total = jnp.zeros((32, policies), jnp.float32)
    for i in range(SLOT):
        ids = jnp.where(row < GROUP, turned[16 * SLOT + i : 16 * SLOT + i + 1], -1.0)
        member = (policy == ids).astype(jnp.bfloat16)
        left = jnp.concatenate([high[16 * i : 16 * i + 16], low[16 * i : 16 * i + 16]], axis=0)
        total = total + lax.dot_general(left, member, NT, preferred_element_type=jnp.float32)
    policy_ground = total[:16] + total[16:]

    pairs = [arrived[2 * k, 24:32, :] + arrived[2 * k + 1, 24:32, :] for k in range(owners // 2)]
    params = jnp.concatenate(pairs, axis=1)
    loss = params[6:7] * jnp.minimum(jnp.maximum(policy_ground - params[4:5], 0.0), params[5:6])
    own = lax.axis_index("pol") * SUMM_DEV
    group = lax.broadcasted_iota(jnp.int32, (8, policies), 0)
    wanted = jnp.where(group < SUMM_DEV, (group + own).astype(jnp.float32), -1.0)
    chosen = (wanted == params[7:8]).astype(jnp.float32)
    spread = jnp.concatenate([loss * chosen[k : k + 1] for k in range(SUMM_DEV)], axis=0)
    high, low = two_terms(jnp.concatenate([spread, jnp.zeros((128 - 16 * SUMM_DEV, policies), jnp.float32)], axis=0))
    ones = jnp.ones((8, policies), jnp.bfloat16)
    sums = lax.dot_general(ones, high, NT, preferred_element_type=jnp.float32) + lax.dot_general(
        ones, low, NT, preferred_element_type=jnp.float32
    )
    shards = out.shape[0] // 3
    lane = lax.broadcasted_iota(jnp.int32, (8, 128), 1)
    sums = jnp.where(lane < 16 * SUMM_DEV, sums, compact[shards : shards + 8, :128])
    for k in range(shards // 8):
        out[pl.ds(24 * k, 8, stride=3), :] = sums
    out[pl.ds(1, shards, stride=3), :] = compact[:shards, :128]
    out[pl.ds(2, shards, stride=3), :] = compact[:shards, 128:]


def all_years_kernel(losses, occurrence, out):
    turned = jnp.concatenate([occurrence[...].astype(jnp.float32).T, jnp.zeros((64, 112), jnp.float32)], axis=1)
    tiles = [turned[8 * r : 8 * r + 8] for r in range(8)]
    tiles = [pltpu.roll(t, 0, 1, stride=16, stride_axis=0) for t in tiles]
    lane = lax.broadcasted_iota(jnp.int32, (1, 128), 1)
    rows = [jnp.where(lane < 16 * SUMM_DEV, losses[0:1, :], 0.0)] + [jnp.sum(t, axis=0, keepdims=True) for t in tiles]
    nine = jnp.concatenate(rows, axis=0)
    for k in range(out.shape[0] // 9):
        out[9 * k : 9 * k + 9, :] = nine


def year_kernel(rows_per_source, whole, arrived, out, flag, uppers, lowers, spread, spare):
    sources = arrived.shape[0] // rows_per_source
    base = (lax.axis_index("ev") * YR_DEV).astype(jnp.float32) if whole else 1.0
    year = arrived[...] - base
    upper = jnp.floor(year * (1.0 / 128.0))
    uppers[...] = upper
    lowers[...] = year - 128.0 * upper

    first = arrived[pl.ds(0, sources, stride=rows_per_source), :]
    flag[0, 0] = (jnp.min(first) < 0.0).astype(jnp.int32)
    high, low = two_terms(first)
    lane = lax.broadcasted_iota(jnp.int32, (128, 128), 1)
    sub = lax.broadcasted_iota(jnp.int32, (128, 128), 0)
    repeat = jnp.concatenate(
        [(sub == lane % 16 + 16 * k).astype(jnp.float32).astype(jnp.bfloat16) for k in range(SUMM_DEV)], axis=1
    )
    spread[...] = jnp.dot(jnp.concatenate([high, low], axis=0), repeat, preferred_element_type=jnp.float32)

    row = sub.astype(jnp.float32).astype(jnp.bfloat16)
    upper_row = (lax.broadcasted_iota(jnp.int32, (16, 128), 0) % 8).astype(jnp.float32).astype(jnp.bfloat16)
    one = jnp.ones((16, 128), jnp.bfloat16)
    zero = jnp.zeros((16, 128), jnp.bfloat16)

    def step(source, total):
        losses = []
        for term in range(2):
            values = spread[pl.ds(term * sources + source, 1), :]
            for k in range(0, SUMM_DEV, 2):
                pair = [jnp.broadcast_to(values[:, 128 * (k + i) : 128 * (k + i) + 128], (8, 128)) for i in range(2)]
                losses.append(jnp.concatenate(pair, axis=0).astype(jnp.bfloat16))
        left, right = [], []
        for r in range(1, rows_per_source):
            at = pl.ds(rows_per_source * source + r, 1)
            upper = jnp.broadcast_to(uppers[at, :], (16, 128)).astype(jnp.bfloat16)
            lower = jnp.broadcast_to(lowers[at, :], (16, 128)).astype(jnp.bfloat16)
            match = upper == upper_row
            right.append(jnp.concatenate([jnp.where(match, x, zero) for x in losses], axis=0))
            left.append(
                jnp.concatenate([jnp.where(row[16 * h : 16 * h + 16] == lower, one, zero) for h in range(8)], axis=0)
            )
        return total + lax.dot_general(
            jnp.concatenate(left, axis=1), jnp.concatenate(right, axis=1), NT, preferred_element_type=jnp.float32
        )

    total = lax.fori_loop(0, sources, step, jnp.zeros((128, 64), jnp.float32), unroll=32 if rows_per_source == 3 else 8).T
    spare[...] = total[:32] + total[32:]
    for h in range(8):
        out[:, 128 * h : 128 * h + 128] = spare[pl.ds(h, SUMM_DEV, stride=8), :]


def per_device(
    ground_up,
    loc_deductible,
    loc_limit,
    block_policy,
    policy_deductible,
    policy_limit,
    policy_share,
    policy_summary,
    occurrence,
):
    owners = lax.axis_size("pol")
    shards = lax.axis_size("ev")
    compiler_params = pltpu.CompilerParams(vmem_limit_bytes=32 * 1024 * 1024)
    payload, compact = pl.pallas_call(
        local_kernel,
        name="local",
        out_shape=(
            jax.ShapeDtypeStruct((owners, 32, 128), jnp.float32),
            jax.ShapeDtypeStruct((shards + 8, 16 * SLOTS), jnp.float32),
        ),
        in_specs=[pl.BlockSpec(memory_space=pltpu.HBM)] * 9,
        out_specs=(VMEM, VMEM),
        scratch_shapes=[
            pltpu.VMEM(ground_up.shape, jnp.bfloat16),
            pltpu.VMEM(loc_deductible.shape, jnp.bfloat16),
            pltpu.VMEM(loc_limit.shape, jnp.bfloat16),
            pltpu.VMEM((1, block_policy.shape[0]), jnp.int32),
            pltpu.VMEM((1, 64), jnp.float32),
            pltpu.VMEM((1, 64), jnp.float32),
            pltpu.VMEM((1, 64), jnp.float32),
            pltpu.VMEM((1, 64), jnp.int32),
            pltpu.VMEM(occurrence.shape, jnp.int32),
            pltpu.VMEM((GROUP // 2, 128, 256), jnp.bfloat16),
            pltpu.VMEM((8, 256), jnp.float32),
            pltpu.VMEM((8, 128), jnp.float32),
            pltpu.SemaphoreType.DMA((2 + SLOT + 6,)),
        ],
        compiler_params=compiler_params,
    )(
        pltpu.with_memory_space_constraint(ground_up, pltpu.HBM),
        pltpu.with_memory_space_constraint(loc_deductible, pltpu.HBM),
        pltpu.with_memory_space_constraint(loc_limit, pltpu.HBM),
        pltpu.with_memory_space_constraint(block_policy[None], pltpu.HBM),
        pltpu.with_memory_space_constraint(policy_deductible[None], pltpu.HBM),
        pltpu.with_memory_space_constraint(policy_limit[None], pltpu.HBM),
        pltpu.with_memory_space_constraint(policy_share[None], pltpu.HBM),
        pltpu.with_memory_space_constraint(policy_summary[None], pltpu.HBM),
        pltpu.with_memory_space_constraint(occurrence, pltpu.HBM),
    )
    arrived = lax.all_to_all(payload, "pol", split_axis=0, concat_axis=0, tiled=True)
    losses = pl.pallas_call(
        policy_kernel,
        name="policies",
        out_shape=jax.ShapeDtypeStruct((3 * shards, 128), jnp.float32),
        in_specs=[VMEM] * 2,
        out_specs=VMEM,
        compiler_params=compiler_params,
    )(arrived, compact)
    arrived = lax.all_to_all(losses.reshape(shards, 1, 3 * 128), "ev", split_axis=0, concat_axis=0, tiled=True)
    arrived = arrived.reshape(3 * shards, 128)

    def add_years(arrived, rows_per_source, whole, name):
        return pl.pallas_call(
            functools.partial(year_kernel, rows_per_source, whole),
            name=name,
            out_shape=(
                jax.ShapeDtypeStruct((SUMM_DEV, YR_DEV), jnp.float32),
                jax.ShapeDtypeStruct((1, 1), jnp.int32),
            ),
            in_specs=[VMEM],
            out_specs=(VMEM, pl.BlockSpec(memory_space=pltpu.SMEM)),
            scratch_shapes=[
                pltpu.VMEM((rows_per_source * shards, 128), jnp.float32),
                pltpu.VMEM((rows_per_source * shards, 128), jnp.float32),
                pltpu.VMEM((2 * shards, 128 * SUMM_DEV), jnp.float32),
                pltpu.VMEM((32, 128), jnp.float32),
            ],
            compiler_params=compiler_params,
        )(arrived)

    def general_case(state):
        losses, occurrence = state[2:]
        payload = pl.pallas_call(
            all_years_kernel,
            name="all_years",
            out_shape=jax.ShapeDtypeStruct((9 * shards, 128), jnp.float32),
            in_specs=[VMEM] * 2,
            out_specs=VMEM,
            compiler_params=compiler_params,
        )(losses, occurrence)
        arrived = lax.all_to_all(payload[:, None], "ev", split_axis=0, concat_axis=0, tiled=True)[:, 0]
        year_loss, _ = add_years(arrived, 9, True, "years_all")
        return year_loss, jnp.zeros((1, 1), jnp.int32), losses, occurrence

    year_loss, flag = add_years(arrived, 3, False, "years")
    state = lax.while_loop(lambda state: state[1][0, 0] > 0, general_case, (year_loss, flag, losses, occurrence))
    return state[0]


def solution(mesh):
    placed = (
        P("pol", "ev", None),
        P("pol", None),
        P("pol", None),
        P("pol"),
        P("pol"),
        P("pol"),
        P("pol"),
        P("pol"),
        P("ev", None),
    )
    return jax.shard_map(
        per_device, mesh=mesh, in_specs=placed, out_specs=P("pol", "ev"), check_vma=False
    )
```

```python
import functools

import jax
import jax.numpy as jnp
from jax import lax
from jax.experimental import pallas as pl
from jax.experimental.pallas import tpu as pltpu
from jax.sharding import PartitionSpec as P

SUMM_DEV = 4
YR_DEV = 1024
FIRST_POL = 4
FIRST_EV = 22
GROUP = 28
SLOT = 7
SLOTS = 16
NT = (((1,), (1,)), ((), ()))
VMEM = pl.BlockSpec(memory_space=pltpu.VMEM)


def two_terms(x):
    high = x.astype(jnp.bfloat16)
    return high, (x - high.astype(jnp.float32)).astype(jnp.bfloat16)


def local_kernel(
    ground_hbm,
    deduct_hbm,
    limit_hbm,
    owner_hbm,
    ded_hbm,
    lim_hbm,
    share_hbm,
    summ_hbm,
    years_hbm,
    out,
    out_years,
    ground,
    deduct,
    limit,
    owner,
    ded,
    lim,
    share,
    summ,
    years,
    terms,
    ids,
    params,
    sems,
):
    blocks = ground.shape[0]
    part = 4 * SLOT
    bounds = [(first, min(part, blocks - first)) for first in range(0, GROUP * SLOT, part)]
    small = [
        (years_hbm, years),
        (owner_hbm, owner),
        (ded_hbm, ded),
        (lim_hbm, lim),
        (share_hbm, share),
        (summ_hbm, summ),
    ]
    pairs = small + [(deduct_hbm, deduct), (limit_hbm, limit)]
    pairs += [(ground_hbm.at[first : first + count], ground.at[first : first + count]) for first, count in bounds]
    copies = [pltpu.make_async_copy(source, target, sems.at[n]) for n, (source, target) in enumerate(pairs)]
    for copy in copies:
        copy.start()
    sub = lax.broadcasted_iota(jnp.int32, (8, 128), 0)
    lane = lax.broadcasted_iota(jnp.int32, (8, 128), 1)
    terms[:, 16 * SLOT :, :] = jnp.zeros((GROUP // 2, 128 - 16 * SLOT, 256), jnp.bfloat16)
    ids[...] = jnp.full((8, 256), -1.0, jnp.float32)
    params[...] = jnp.zeros((8, 128), jnp.float32)
    for copy in copies[: len(small)]:
        copy.wait()

    half_members, key, code, over = rank_years(years)
    ids[0:1, 0:blocks] = owner[...].astype(jnp.float32)
    block = lax.broadcasted_iota(jnp.int32, (32, 256), 1).astype(jnp.float32)
    at_row = jnp.floor((block + 0.5) * (1.0 / SLOT)) == lax.broadcasted_iota(jnp.int32, (32, 256), 0).astype(jnp.float32)
    policy = ids[0:1, :]
    upper = 256.0 * jnp.floor(policy * (1.0 / 256.0))
    left = jnp.concatenate([jnp.where(at_row, upper, 0.0), jnp.where(at_row, policy - upper, 0.0)], axis=0)
    block = lax.broadcasted_iota(jnp.int32, (256, 128), 0).astype(jnp.float32)
    block = block - SLOT * jnp.floor((block + 0.5) * (1.0 / SLOT))
    right = block + 16.0 * SLOT == lax.broadcasted_iota(jnp.int32, (256, 128), 1).astype(jnp.float32)
    columns = jnp.dot(
        left.astype(jnp.bfloat16), right.astype(jnp.float32).astype(jnp.bfloat16), preferred_element_type=jnp.float32
    )
    columns = columns[:32] + columns[32:]
    params[4:5, 0:64] = ded[...]
    params[5:6, 0:64] = lim[...]
    params[6:7, 0:64] = share[...]
    params[7:8, 0:64] = summ[...].astype(jnp.float32)
    own = params[...]
    half = lax.rem(lax.axis_index("pol"), 2)
    own = jnp.where(lane // 64 == half, own + pltpu.roll(own, 64, 1), 0.0)

    for copy in copies[len(small) :]:
        copy.wait()
    out_years[...] = place_years(half_members, key, code, over)
    parity = lax.broadcasted_iota(jnp.int32, (8, 256), 0) % 2
    side = (lax.broadcasted_iota(jnp.int32, (8, 256), 1) // 64) % 2
    ones = (parity == side).astype(jnp.float32).astype(jnp.bfloat16)
    low_lanes = lax.broadcasted_iota(jnp.int32, (1, SLOT, 16, 128), 3) < 64
    tiles = [jnp.zeros((8, 128), jnp.float32) for _ in range(4)]
    for c, (first, count) in enumerate(bounds):
        lower = deduct[first : first + count].astype(jnp.float32)[:, None, :]
        upper = limit[first : first + count].astype(jnp.float32)[:, None, :]
        net = jnp.minimum(jnp.maximum(ground[first : first + count].astype(jnp.float32) - lower, 0.0), upper)
        net = net + pltpu.roll(net.reshape(16 * count, 128), 64, 1).reshape(net.shape)
        if count < part:
            net = jnp.concatenate([net, jnp.zeros((part - count, 16, 128), jnp.float32)], axis=0)
        net = net.reshape(2, 2, SLOT, 16, 128)
        both = jnp.where(low_lanes, net[:, 0], net[:, 1])
        for term, value in enumerate(two_terms(both)):
            terms[2 * c : 2 * c + 2, : 16 * SLOT, 128 * term : 128 * term + 128] = value.reshape(2, 16 * SLOT, 128)
        weights = terms[2 * c : 2 * c + 2].reshape(256, 256)
        sums = lax.dot_general(ones, weights, NT, preferred_element_type=jnp.float32)
        for n in (2 * c, 2 * c + 1):
            piece = sums[:, 128 * (n % 2) : 128 * (n % 2) + 128]
            tiles[n // 4] = jnp.where(sub // 2 == n % 4, piece, tiles[n // 4])
    tiles = [tiles[t] + columns[8 * t : 8 * t + 8] for t in range(4)]
    tiles[3] = jnp.where(sub < 4, tiles[3], own)
    for t in range(4):
        for k in range(out.shape[0]):
            out[k, 8 * t : 8 * t + 8, :] = tiles[t]


def rank_years(years):
    shards = 32
    year = jnp.concatenate([years[pl.ds(0, 8, stride=2), :], years[pl.ds(1, 8, stride=2), :]], axis=1).astype(jnp.float32)
    shard = jnp.floor(year * (1.0 / YR_DEV))
    code = year - YR_DEV * shard + 1.0
    shard_row = ((lax.broadcasted_iota(jnp.int32, (shards, 128), 0) + FIRST_EV) % shards).astype(jnp.float32)
    member = [(shard_row == shard[r : r + 1]).astype(jnp.float32) for r in range(8)]
    half = [jnp.concatenate([member[2 * j], member[2 * j + 1]], axis=1) for j in range(4)]
    first = lax.broadcasted_iota(jnp.int32, (256, 256), 0)
    second = lax.broadcasted_iota(jnp.int32, (256, 256), 1)
    before = ((first // 64 == second // 64) & (first < second)).astype(jnp.float32).astype(jnp.bfloat16)
    stacked = jnp.concatenate(half, axis=0)
    ahead = jnp.dot(stacked.astype(jnp.bfloat16), before, preferred_element_type=jnp.float32)
    rank = jnp.sum((stacked * ahead).reshape(4, shards, 256), axis=1)
    event = lax.broadcasted_iota(jnp.int32, (4, 256), 1) // 64 + 4 * lax.broadcasted_iota(jnp.int32, (4, 256), 0)
    key = 16.0 * rank + event.astype(jnp.float32)
    most = jnp.max(jnp.max(rank, axis=0, keepdims=True), axis=1, keepdims=True)
    return jnp.concatenate(half, axis=1).astype(jnp.bfloat16), key, code, jnp.where(most >= SLOTS, -1.0, 0.0)


def place_years(members, key, code, over):
    slot_row = lax.broadcasted_iota(jnp.int32, (16 * SLOTS, 256), 0).astype(jnp.float32)
    upper = jnp.floor(code * (1.0 / 16.0))
    sums = []
    for value in (upper, code - 16.0 * upper):
        right = []
        for j in range(4):
            flat = jnp.concatenate([value[2 * j : 2 * j + 1], value[2 * j + 1 : 2 * j + 2]], axis=1)
            right.append(jnp.where(slot_row == key[j : j + 1], flat, 0.0).astype(jnp.bfloat16))
        sums.append(lax.dot_general(members, jnp.concatenate(right, axis=1), NT, preferred_element_type=jnp.float32))
    return jnp.concatenate([16.0 * sums[0] + sums[1], jnp.broadcast_to(over, (8, 16 * SLOTS))], axis=0)


def policy_kernel(arrived, compact, out):
    owners = arrived.shape[0]
    policies = 64 * owners
    flat = arrived[...].reshape(owners * 32, 128)
    turned = flat.T
    row = lax.broadcasted_iota(jnp.int32, (1, owners * 32), 1) % 32
    high, low = two_terms(turned[: 16 * SLOT])
    policy = lax.broadcasted_iota(jnp.int32, (policies, owners * 32), 0)
    policy = ((policy + 64 * FIRST_POL) % policies).astype(jnp.float32)
    total = jnp.zeros((32, policies), jnp.float32)
    for i in range(SLOT):
        ids = jnp.where(row < GROUP, turned[16 * SLOT + i : 16 * SLOT + i + 1], -1.0)
        member = (policy == ids).astype(jnp.bfloat16)
        left = jnp.concatenate([high[16 * i : 16 * i + 16], low[16 * i : 16 * i + 16]], axis=0)
        total = total + lax.dot_general(left, member, NT, preferred_element_type=jnp.float32)
    policy_ground = total[:16] + total[16:]

    pairs = [arrived[2 * k, 24:32, :] + arrived[2 * k + 1, 24:32, :] for k in range(owners // 2)]
    params = jnp.concatenate(pairs, axis=1)
    loss = params[6:7] * jnp.minimum(jnp.maximum(policy_ground - params[4:5], 0.0), params[5:6])
    own = lax.axis_index("pol") * SUMM_DEV
    group = lax.broadcasted_iota(jnp.int32, (8, policies), 0)
    wanted = jnp.where(group < SUMM_DEV, (group + own).astype(jnp.float32), -1.0)
    chosen = (wanted == params[7:8]).astype(jnp.float32)
    spread = jnp.concatenate([loss * chosen[k : k + 1] for k in range(SUMM_DEV)], axis=0)
    high, low = two_terms(jnp.concatenate([spread, jnp.zeros((128 - 16 * SUMM_DEV, policies), jnp.float32)], axis=0))
    ones = jnp.ones((8, policies), jnp.bfloat16)
    sums = lax.dot_general(ones, high, NT, preferred_element_type=jnp.float32) + lax.dot_general(
        ones, low, NT, preferred_element_type=jnp.float32
    )
    shards = out.shape[0] // 3
    lane = lax.broadcasted_iota(jnp.int32, (8, 128), 1)
    sums = jnp.where(lane < 16 * SUMM_DEV, sums, compact[shards : shards + 8, :128])
    for k in range(shards // 8):
        out[pl.ds(24 * k, 8, stride=3), :] = sums
    out[pl.ds(1, shards, stride=3), :] = compact[:shards, :128]
    out[pl.ds(2, shards, stride=3), :] = compact[:shards, 128:]


def all_years_kernel(losses, occurrence, out):
    turned = jnp.concatenate([occurrence[...].astype(jnp.float32).T, jnp.zeros((64, 112), jnp.float32)], axis=1)
    tiles = [turned[8 * r : 8 * r + 8] for r in range(8)]
    tiles = [pltpu.roll(t, 0, 1, stride=16, stride_axis=0) for t in tiles]
    lane = lax.broadcasted_iota(jnp.int32, (1, 128), 1)
    rows = [jnp.where(lane < 16 * SUMM_DEV, losses[0:1, :], 0.0)] + [jnp.sum(t, axis=0, keepdims=True) for t in tiles]
    nine = jnp.concatenate(rows, axis=0)
    for k in range(out.shape[0] // 9):
        out[9 * k : 9 * k + 9, :] = nine


def year_kernel(rows_per_source, whole, arrived, out, flag, uppers, lowers, spread, spare):
    sources = arrived.shape[0] // rows_per_source
    base = (lax.axis_index("ev") * YR_DEV).astype(jnp.float32) if whole else 1.0
    year = arrived[...] - base
    upper = jnp.floor(year * (1.0 / 128.0))
    uppers[...] = upper
    lowers[...] = year - 128.0 * upper

    first = arrived[pl.ds(0, sources, stride=rows_per_source), :]
    flag[0, 0] = (jnp.min(first) < 0.0).astype(jnp.int32)
    high, low = two_terms(first)
    lane = lax.broadcasted_iota(jnp.int32, (128, 128), 1)
    sub = lax.broadcasted_iota(jnp.int32, (128, 128), 0)
    repeat = jnp.concatenate(
        [(sub == lane % 16 + 16 * k).astype(jnp.float32).astype(jnp.bfloat16) for k in range(SUMM_DEV)], axis=1
    )
    spread[...] = jnp.dot(jnp.concatenate([high, low], axis=0), repeat, preferred_element_type=jnp.float32)

    row = sub.astype(jnp.float32).astype(jnp.bfloat16)
    upper_row = (lax.broadcasted_iota(jnp.int32, (16, 128), 0) % 8).astype(jnp.float32).astype(jnp.bfloat16)
    one = jnp.ones((16, 128), jnp.bfloat16)
    zero = jnp.zeros((16, 128), jnp.bfloat16)

    def step(source, total):
        losses = []
        for term in range(2):
            values = spread[pl.ds(term * sources + source, 1), :]
            for k in range(0, SUMM_DEV, 2):
                pair = [jnp.broadcast_to(values[:, 128 * (k + i) : 128 * (k + i) + 128], (8, 128)) for i in range(2)]
                losses.append(jnp.concatenate(pair, axis=0).astype(jnp.bfloat16))
        left, right = [], []
        for r in range(1, rows_per_source):
            at = pl.ds(rows_per_source * source + r, 1)
            upper = jnp.broadcast_to(uppers[at, :], (16, 128)).astype(jnp.bfloat16)
            lower = jnp.broadcast_to(lowers[at, :], (16, 128)).astype(jnp.bfloat16)
            match = upper == upper_row
            right.append(jnp.concatenate([jnp.where(match, x, zero) for x in losses], axis=0))
            left.append(
                jnp.concatenate([jnp.where(row[16 * h : 16 * h + 16] == lower, one, zero) for h in range(8)], axis=0)
            )
        return total + lax.dot_general(
            jnp.concatenate(left, axis=1), jnp.concatenate(right, axis=1), NT, preferred_element_type=jnp.float32
        )

    total = lax.fori_loop(0, sources, step, jnp.zeros((128, 64), jnp.float32), unroll=32 if rows_per_source == 3 else 8).T
    spare[...] = total[:32] + total[32:]
    for h in range(8):
        out[:, 128 * h : 128 * h + 128] = spare[pl.ds(h, SUMM_DEV, stride=8), :]


def per_device(
    ground_up,
    loc_deductible,
    loc_limit,
    block_policy,
    policy_deductible,
    policy_limit,
    policy_share,
    policy_summary,
    occurrence,
):
    owners = lax.axis_size("pol")
    shards = lax.axis_size("ev")
    compiler_params = pltpu.CompilerParams(vmem_limit_bytes=32 * 1024 * 1024)
    payload, compact = pl.pallas_call(
        local_kernel,
        name="local",
        out_shape=(
            jax.ShapeDtypeStruct((owners, 32, 128), jnp.float32),
            jax.ShapeDtypeStruct((shards + 8, 16 * SLOTS), jnp.float32),
        ),
        in_specs=[pl.BlockSpec(memory_space=pltpu.HBM)] * 9,
        out_specs=(VMEM, VMEM),
        scratch_shapes=[
            pltpu.VMEM(ground_up.shape, jnp.bfloat16),
            pltpu.VMEM(loc_deductible.shape, jnp.bfloat16),
            pltpu.VMEM(loc_limit.shape, jnp.bfloat16),
            pltpu.VMEM((1, block_policy.shape[0]), jnp.int32),
            pltpu.VMEM((1, 64), jnp.float32),
            pltpu.VMEM((1, 64), jnp.float32),
            pltpu.VMEM((1, 64), jnp.float32),
            pltpu.VMEM((1, 64), jnp.int32),
            pltpu.VMEM(occurrence.shape, jnp.int32),
            pltpu.VMEM((GROUP // 2, 128, 256), jnp.bfloat16),
            pltpu.VMEM((8, 256), jnp.float32),
            pltpu.VMEM((8, 128), jnp.float32),
            pltpu.SemaphoreType.DMA((2 + SLOT + 6,)),
        ],
        compiler_params=compiler_params,
    )(
        pltpu.with_memory_space_constraint(ground_up, pltpu.HBM),
        pltpu.with_memory_space_constraint(loc_deductible, pltpu.HBM),
        pltpu.with_memory_space_constraint(loc_limit, pltpu.HBM),
        pltpu.with_memory_space_constraint(block_policy[None], pltpu.HBM),
        pltpu.with_memory_space_constraint(policy_deductible[None], pltpu.HBM),
        pltpu.with_memory_space_constraint(policy_limit[None], pltpu.HBM),
        pltpu.with_memory_space_constraint(policy_share[None], pltpu.HBM),
        pltpu.with_memory_space_constraint(policy_summary[None], pltpu.HBM),
        pltpu.with_memory_space_constraint(occurrence, pltpu.HBM),
    )
    order = [[(i + FIRST_POL) % owners for i in range(owners)]]
    arrived = lax.all_to_all(payload, "pol", split_axis=0, concat_axis=0, axis_index_groups=order, tiled=True)
    losses = pl.pallas_call(
        policy_kernel,
        name="policies",
        out_shape=jax.ShapeDtypeStruct((3 * shards, 128), jnp.float32),
        in_specs=[VMEM] * 2,
        out_specs=VMEM,
        compiler_params=compiler_params,
    )(arrived, compact)
    order = [[(i + FIRST_EV) % shards for i in range(shards)]]
    arrived = lax.all_to_all(
        losses.reshape(shards, 1, 3 * 128), "ev", split_axis=0, concat_axis=0, axis_index_groups=order, tiled=True
    )
    arrived = arrived.reshape(3 * shards, 128)

    def add_years(arrived, rows_per_source, whole, name):
        return pl.pallas_call(
            functools.partial(year_kernel, rows_per_source, whole),
            name=name,
            out_shape=(
                jax.ShapeDtypeStruct((SUMM_DEV, YR_DEV), jnp.float32),
                jax.ShapeDtypeStruct((1, 1), jnp.int32),
            ),
            in_specs=[VMEM],
            out_specs=(VMEM, pl.BlockSpec(memory_space=pltpu.SMEM)),
            scratch_shapes=[
                pltpu.VMEM((rows_per_source * shards, 128), jnp.float32),
                pltpu.VMEM((rows_per_source * shards, 128), jnp.float32),
                pltpu.VMEM((2 * shards, 128 * SUMM_DEV), jnp.float32),
                pltpu.VMEM((32, 128), jnp.float32),
            ],
            compiler_params=compiler_params,
        )(arrived)

    def general_case(state):
        losses, occurrence = state[2:]
        payload = pl.pallas_call(
            all_years_kernel,
            name="all_years",
            out_shape=jax.ShapeDtypeStruct((9 * shards, 128), jnp.float32),
            in_specs=[VMEM] * 2,
            out_specs=VMEM,
            compiler_params=compiler_params,
        )(losses, occurrence)
        arrived = lax.all_to_all(payload[:, None], "ev", split_axis=0, concat_axis=0, tiled=True)[:, 0]
        year_loss, _ = add_years(arrived, 9, True, "years_all")
        return year_loss, jnp.zeros((1, 1), jnp.int32), losses, occurrence

    year_loss, flag = add_years(arrived, 3, False, "years")
    state = lax.while_loop(lambda state: state[1][0, 0] > 0, general_case, (year_loss, flag, losses, occurrence))
    return state[0]


def solution(mesh):
    placed = (
        P("pol", "ev", None),
        P("pol", None),
        P("pol", None),
        P("pol"),
        P("pol"),
        P("pol"),
        P("pol"),
        P("pol"),
        P("ev", None),
    )
    return jax.shard_map(
        per_device, mesh=mesh, in_specs=placed, out_specs=P("pol", "ev"), check_vma=False
    )
```

```python
import functools

import jax
import jax.numpy as jnp
from jax import lax
from jax.experimental import pallas as pl
from jax.experimental.pallas import tpu as pltpu
from jax.sharding import PartitionSpec as P

SUMM_DEV = 4
YR_DEV = 1024
FIRST_POL = 4
FIRST_EV = 22
GROUP = 28
SLOT = 7
SLOTS = 16
NT = (((1,), (1,)), ((), ()))
VMEM = pl.BlockSpec(memory_space=pltpu.VMEM)


def two_terms(x):
    high = x.astype(jnp.bfloat16)
    return high, (x - high.astype(jnp.float32)).astype(jnp.bfloat16)


def local_kernel(
    ground_hbm,
    deduct_hbm,
    limit_hbm,
    owner_hbm,
    ded_hbm,
    lim_hbm,
    share_hbm,
    summ_hbm,
    years_hbm,
    out,
    out_years,
    ground,
    deduct,
    limit,
    owner,
    ded,
    lim,
    share,
    summ,
    years,
    terms,
    ids,
    params,
    sems,
):
    blocks = ground.shape[0]
    part = 4 * SLOT
    bounds = [(first, min(part, blocks - first)) for first in range(0, GROUP * SLOT, part)]
    small = [
        (years_hbm, years),
        (owner_hbm, owner),
        (ded_hbm, ded),
        (lim_hbm, lim),
        (share_hbm, share),
        (summ_hbm, summ),
    ]
    pairs = small + [(ground_hbm, ground), (deduct_hbm, deduct), (limit_hbm, limit)]
    copies = [pltpu.make_async_copy(source, target, sems.at[n]) for n, (source, target) in enumerate(pairs)]
    for copy in copies:
        copy.start()
    sub = lax.broadcasted_iota(jnp.int32, (8, 128), 0)
    lane = lax.broadcasted_iota(jnp.int32, (8, 128), 1)
    terms[:, 16 * SLOT :, :] = jnp.zeros((GROUP // 2, 128 - 16 * SLOT, 256), jnp.bfloat16)
    ids[...] = jnp.full((8, 256), -1.0, jnp.float32)
    params[...] = jnp.zeros((8, 128), jnp.float32)
    for copy in copies[: len(small)]:
        copy.wait()

    half_members, key, code, over = rank_years(years)
    ids[0:1, 0:blocks] = owner[...].astype(jnp.float32)
    block = lax.broadcasted_iota(jnp.int32, (32, 256), 1).astype(jnp.float32)
    at_row = jnp.floor((block + 0.5) * (1.0 / SLOT)) == lax.broadcasted_iota(jnp.int32, (32, 256), 0).astype(jnp.float32)
    policy = ids[0:1, :]
    upper = 256.0 * jnp.floor(policy * (1.0 / 256.0))
    left = jnp.concatenate([jnp.where(at_row, upper, 0.0), jnp.where(at_row, policy - upper, 0.0)], axis=0)
    block = lax.broadcasted_iota(jnp.int32, (256, 128), 0).astype(jnp.float32)
    block = block - SLOT * jnp.floor((block + 0.5) * (1.0 / SLOT))
    right = block + 16.0 * SLOT == lax.broadcasted_iota(jnp.int32, (256, 128), 1).astype(jnp.float32)
    columns = jnp.dot(
        left.astype(jnp.bfloat16), right.astype(jnp.float32).astype(jnp.bfloat16), preferred_element_type=jnp.float32
    )
    columns = columns[:32] + columns[32:]
    params[4:5, 0:64] = ded[...]
    params[5:6, 0:64] = lim[...]
    params[6:7, 0:64] = share[...]
    params[7:8, 0:64] = summ[...].astype(jnp.float32)
    own = params[...]

    for copy in copies[len(small) :]:
        copy.wait()
    out_years[...] = place_years(half_members, key, code, over)
    parity = lax.broadcasted_iota(jnp.int32, (8, 256), 0) % 2
    side = (lax.broadcasted_iota(jnp.int32, (8, 256), 1) // 64) % 2
    ones = (parity == side).astype(jnp.float32).astype(jnp.bfloat16)
    low_lanes = lax.broadcasted_iota(jnp.int32, (1, SLOT, 16, 128), 3) < 64
    tiles = [jnp.zeros((8, 128), jnp.float32) for _ in range(4)]
    for c, (first, count) in enumerate(bounds):
        lower = deduct[first : first + count].astype(jnp.float32)[:, None, :]
        upper = limit[first : first + count].astype(jnp.float32)[:, None, :]
        net = jnp.minimum(jnp.maximum(ground[first : first + count].astype(jnp.float32) - lower, 0.0), upper)
        net = net + pltpu.roll(net.reshape(16 * count, 128), 64, 1).reshape(net.shape)
        if count < part:
            net = jnp.concatenate([net, jnp.zeros((part - count, 16, 128), jnp.float32)], axis=0)
        net = net.reshape(2, 2, SLOT, 16, 128)
        both = jnp.where(low_lanes, net[:, 0], net[:, 1])
        for term, value in enumerate(two_terms(both)):
            terms[2 * c : 2 * c + 2, : 16 * SLOT, 128 * term : 128 * term + 128] = value.reshape(2, 16 * SLOT, 128)
        weights = terms[2 * c : 2 * c + 2].reshape(256, 256)
        sums = lax.dot_general(ones, weights, NT, preferred_element_type=jnp.float32)
        for n in (2 * c, 2 * c + 1):
            piece = sums[:, 128 * (n % 2) : 128 * (n % 2) + 128]
            tiles[n // 4] = jnp.where(sub // 2 == n % 4, piece, tiles[n // 4])
    tiles = [tiles[t] + columns[8 * t : 8 * t + 8] for t in range(4)]
    tiles[3] = jnp.where(sub < 4, tiles[3], own)
    for t in range(4):
        for k in range(out.shape[0]):
            out[k, 8 * t : 8 * t + 8, :] = tiles[t]


def rank_years(years):
    shards = 32
    year = jnp.concatenate([years[pl.ds(0, 8, stride=2), :], years[pl.ds(1, 8, stride=2), :]], axis=1).astype(jnp.float32)
    shard = jnp.floor(year * (1.0 / YR_DEV))
    code = year - YR_DEV * shard + 1.0
    shard_row = ((lax.broadcasted_iota(jnp.int32, (shards, 128), 0) + FIRST_EV) % shards).astype(jnp.float32)
    member = [(shard_row == shard[r : r + 1]).astype(jnp.float32) for r in range(8)]
    half = [jnp.concatenate([member[2 * j], member[2 * j + 1]], axis=1) for j in range(4)]
    first = lax.broadcasted_iota(jnp.int32, (256, 256), 0)
    second = lax.broadcasted_iota(jnp.int32, (256, 256), 1)
    before = ((first // 64 == second // 64) & (first < second)).astype(jnp.float32).astype(jnp.bfloat16)
    stacked = jnp.concatenate(half, axis=0)
    ahead = jnp.dot(stacked.astype(jnp.bfloat16), before, preferred_element_type=jnp.float32)
    rank = jnp.sum((stacked * ahead).reshape(4, shards, 256), axis=1)
    event = lax.broadcasted_iota(jnp.int32, (4, 256), 1) // 64 + 4 * lax.broadcasted_iota(jnp.int32, (4, 256), 0)
    key = 16.0 * rank + event.astype(jnp.float32)
    most = jnp.max(jnp.max(rank, axis=0, keepdims=True), axis=1, keepdims=True)
    return jnp.concatenate(half, axis=1).astype(jnp.bfloat16), key, code, jnp.where(most >= SLOTS, -1.0, 0.0)


def place_years(members, key, code, over):
    slot_row = lax.broadcasted_iota(jnp.int32, (16 * SLOTS, 256), 0).astype(jnp.float32)
    upper = jnp.floor(code * (1.0 / 16.0))
    sums = []
    for value in (upper, code - 16.0 * upper):
        right = []
        for j in range(4):
            flat = jnp.concatenate([value[2 * j : 2 * j + 1], value[2 * j + 1 : 2 * j + 2]], axis=1)
            right.append(jnp.where(slot_row == key[j : j + 1], flat, 0.0).astype(jnp.bfloat16))
        sums.append(lax.dot_general(members, jnp.concatenate(right, axis=1), NT, preferred_element_type=jnp.float32))
    return jnp.concatenate([16.0 * sums[0] + sums[1], jnp.broadcast_to(over, (8, 16 * SLOTS))], axis=0)


def policy_kernel(arrived, compact, out):
    owners = arrived.shape[0]
    width = owners * 32
    turned = arrived[...].reshape(width, 128).T
    row = lax.broadcasted_iota(jnp.int32, (1, width), 1) % 32
    high, low = two_terms(turned[: 16 * SLOT])
    local_row = lax.broadcasted_iota(jnp.int32, (64, width), 0).astype(jnp.float32).astype(jnp.bfloat16)
    one = jnp.ones((16, width), jnp.bfloat16)
    zero = jnp.zeros((16, width), jnp.bfloat16)
    left, right = [], []
    for i in range(SLOT):
        policy = jnp.where(row < GROUP, turned[16 * SLOT + i : 16 * SLOT + i + 1], -1.0)
        owner = jnp.floor(policy * (1.0 / 64.0))
        local = jnp.broadcast_to(policy - 64.0 * owner, (16, width)).astype(jnp.bfloat16)
        owner = jnp.broadcast_to(owner, (16, width)).astype(jnp.bfloat16)
        terms = [x[16 * i : 16 * i + 16] for x in (high, low)]
        masked = [jnp.where(owner == jnp.bfloat16(o), x, zero) for o in range(owners) for x in terms]
        left.append(jnp.concatenate(masked, axis=0))
        member = [jnp.where(local_row[16 * h : 16 * h + 16] == local, one, zero) for h in range(4)]
        right.append(jnp.concatenate(member, axis=0))
    total = lax.dot_general(
        jnp.concatenate(left, axis=1), jnp.concatenate(right, axis=1), NT, preferred_element_type=jnp.float32
    )

    own = lax.axis_index("pol") * SUMM_DEV
    losses = [jnp.zeros((16, 64), jnp.float32) for _ in range(SUMM_DEV)]
    for o in range(owners):
        policy_ground = total[32 * o : 32 * o + 16] + total[32 * o + 16 : 32 * o + 32]
        place = (o - FIRST_POL) % owners
        ded, lim, share, summ = [arrived[place, GROUP + n : GROUP + n + 1, 0:64] for n in range(4)]
        loss = share * jnp.minimum(jnp.maximum(policy_ground - ded, 0.0), lim)
        for k in range(SUMM_DEV):
            losses[k] = losses[k] + jnp.where(summ == (own + k).astype(jnp.float32), loss, 0.0)
    losses = jnp.concatenate(losses, axis=0)
    losses = jnp.concatenate([losses, jnp.zeros((128 - 16 * SUMM_DEV, 64), jnp.float32)], axis=0)
    ones = jnp.ones((8, 128), jnp.bfloat16)
    weights = jnp.concatenate(two_terms(losses), axis=1)
    sums = lax.dot_general(ones, weights, NT, preferred_element_type=jnp.float32)
    shards = out.shape[0] // 3
    lane = lax.broadcasted_iota(jnp.int32, (8, 128), 1)
    sums = jnp.where(lane < 16 * SUMM_DEV, sums, compact[shards : shards + 8, :128])
    for k in range(shards // 8):
        out[pl.ds(24 * k, 8, stride=3), :] = sums
    out[pl.ds(1, shards, stride=3), :] = compact[:shards, :128]
    out[pl.ds(2, shards, stride=3), :] = compact[:shards, 128:]


def all_years_kernel(losses, occurrence, out):
    turned = jnp.concatenate([occurrence[...].astype(jnp.float32).T, jnp.zeros((64, 112), jnp.float32)], axis=1)
    tiles = [turned[8 * r : 8 * r + 8] for r in range(8)]
    tiles = [pltpu.roll(t, 0, 1, stride=16, stride_axis=0) for t in tiles]
    lane = lax.broadcasted_iota(jnp.int32, (1, 128), 1)
    rows = [jnp.where(lane < 16 * SUMM_DEV, losses[0:1, :], 0.0)] + [jnp.sum(t, axis=0, keepdims=True) for t in tiles]
    nine = jnp.concatenate(rows, axis=0)
    for k in range(out.shape[0] // 9):
        out[9 * k : 9 * k + 9, :] = nine


def year_kernel(rows_per_source, whole, arrived, out, flag, uppers, lowers, spread, spare):
    sources = arrived.shape[0] // rows_per_source
    base = (lax.axis_index("ev") * YR_DEV).astype(jnp.float32) if whole else 1.0
    year = arrived[...] - base
    upper = jnp.floor(year * (1.0 / 128.0))
    uppers[...] = upper
    lowers[...] = year - 128.0 * upper

    first = arrived[pl.ds(0, sources, stride=rows_per_source), :]
    flag[0, 0] = (jnp.min(first) < 0.0).astype(jnp.int32)
    high, low = two_terms(first)
    lane = lax.broadcasted_iota(jnp.int32, (128, 128), 1)
    sub = lax.broadcasted_iota(jnp.int32, (128, 128), 0)
    repeat = jnp.concatenate(
        [(sub == lane % 16 + 16 * k).astype(jnp.float32).astype(jnp.bfloat16) for k in range(SUMM_DEV)], axis=1
    )
    spread[...] = jnp.dot(jnp.concatenate([high, low], axis=0), repeat, preferred_element_type=jnp.float32)

    row = sub.astype(jnp.float32).astype(jnp.bfloat16)
    upper_row = (lax.broadcasted_iota(jnp.int32, (16, 128), 0) % 8).astype(jnp.float32).astype(jnp.bfloat16)
    one = jnp.ones((16, 128), jnp.bfloat16)
    zero = jnp.zeros((16, 128), jnp.bfloat16)

    def step(source, total):
        losses = []
        for term in range(2):
            values = spread[pl.ds(term * sources + source, 1), :]
            for k in range(0, SUMM_DEV, 2):
                pair = [jnp.broadcast_to(values[:, 128 * (k + i) : 128 * (k + i) + 128], (8, 128)) for i in range(2)]
                losses.append(jnp.concatenate(pair, axis=0).astype(jnp.bfloat16))
        left, right = [], []
        for r in range(1, rows_per_source):
            at = pl.ds(rows_per_source * source + r, 1)
            upper = jnp.broadcast_to(uppers[at, :], (16, 128)).astype(jnp.bfloat16)
            lower = jnp.broadcast_to(lowers[at, :], (16, 128)).astype(jnp.bfloat16)
            match = upper == upper_row
            right.append(jnp.concatenate([jnp.where(match, x, zero) for x in losses], axis=0))
            left.append(
                jnp.concatenate([jnp.where(row[16 * h : 16 * h + 16] == lower, one, zero) for h in range(8)], axis=0)
            )
        return total + lax.dot_general(
            jnp.concatenate(left, axis=1), jnp.concatenate(right, axis=1), NT, preferred_element_type=jnp.float32
        )

    total = lax.fori_loop(0, sources, step, jnp.zeros((128, 64), jnp.float32), unroll=32 if rows_per_source == 3 else 8).T
    spare[...] = total[:32] + total[32:]
    for h in range(8):
        out[:, 128 * h : 128 * h + 128] = spare[pl.ds(h, SUMM_DEV, stride=8), :]


def per_device(
    ground_up,
    loc_deductible,
    loc_limit,
    block_policy,
    policy_deductible,
    policy_limit,
    policy_share,
    policy_summary,
    occurrence,
):
    owners = lax.axis_size("pol")
    shards = lax.axis_size("ev")
    compiler_params = pltpu.CompilerParams(vmem_limit_bytes=32 * 1024 * 1024)
    payload, compact = pl.pallas_call(
        local_kernel,
        name="local",
        out_shape=(
            jax.ShapeDtypeStruct((owners, 32, 128), jnp.float32),
            jax.ShapeDtypeStruct((shards + 8, 16 * SLOTS), jnp.float32),
        ),
        in_specs=[pl.BlockSpec(memory_space=pltpu.HBM)] * 9,
        out_specs=(VMEM, VMEM),
        scratch_shapes=[
            pltpu.VMEM(ground_up.shape, jnp.bfloat16),
            pltpu.VMEM(loc_deductible.shape, jnp.bfloat16),
            pltpu.VMEM(loc_limit.shape, jnp.bfloat16),
            pltpu.VMEM((1, block_policy.shape[0]), jnp.int32),
            pltpu.VMEM((1, 64), jnp.float32),
            pltpu.VMEM((1, 64), jnp.float32),
            pltpu.VMEM((1, 64), jnp.float32),
            pltpu.VMEM((1, 64), jnp.int32),
            pltpu.VMEM(occurrence.shape, jnp.int32),
            pltpu.VMEM((GROUP // 2, 128, 256), jnp.bfloat16),
            pltpu.VMEM((8, 256), jnp.float32),
            pltpu.VMEM((8, 128), jnp.float32),
            pltpu.SemaphoreType.DMA((9,)),
        ],
        compiler_params=compiler_params,
    )(
        pltpu.with_memory_space_constraint(ground_up, pltpu.HBM),
        pltpu.with_memory_space_constraint(loc_deductible, pltpu.HBM),
        pltpu.with_memory_space_constraint(loc_limit, pltpu.HBM),
        pltpu.with_memory_space_constraint(block_policy[None], pltpu.HBM),
        pltpu.with_memory_space_constraint(policy_deductible[None], pltpu.HBM),
        pltpu.with_memory_space_constraint(policy_limit[None], pltpu.HBM),
        pltpu.with_memory_space_constraint(policy_share[None], pltpu.HBM),
        pltpu.with_memory_space_constraint(policy_summary[None], pltpu.HBM),
        pltpu.with_memory_space_constraint(occurrence, pltpu.HBM),
    )
    order = [[(i + FIRST_POL) % owners for i in range(owners)]]
    arrived = lax.all_to_all(payload, "pol", split_axis=0, concat_axis=0, axis_index_groups=order, tiled=True)
    losses = pl.pallas_call(
        policy_kernel,
        name="policies",
        out_shape=jax.ShapeDtypeStruct((3 * shards, 128), jnp.float32),
        in_specs=[VMEM] * 2,
        out_specs=VMEM,
        compiler_params=compiler_params,
    )(arrived, compact)
    order = [[(i + FIRST_EV) % shards for i in range(shards)]]
    arrived = lax.all_to_all(
        losses.reshape(shards, 1, 3 * 128), "ev", split_axis=0, concat_axis=0, axis_index_groups=order, tiled=True
    )
    arrived = arrived.reshape(3 * shards, 128)

    def add_years(arrived, rows_per_source, whole, name):
        return pl.pallas_call(
            functools.partial(year_kernel, rows_per_source, whole),
            name=name,
            out_shape=(
                jax.ShapeDtypeStruct((SUMM_DEV, YR_DEV), jnp.float32),
                jax.ShapeDtypeStruct((1, 1), jnp.int32),
            ),
            in_specs=[VMEM],
            out_specs=(VMEM, pl.BlockSpec(memory_space=pltpu.SMEM)),
            scratch_shapes=[
                pltpu.VMEM((rows_per_source * shards, 128), jnp.float32),
                pltpu.VMEM((rows_per_source * shards, 128), jnp.float32),
                pltpu.VMEM((2 * shards, 128 * SUMM_DEV), jnp.float32),
                pltpu.VMEM((32, 128), jnp.float32),
            ],
            compiler_params=compiler_params,
        )(arrived)

    def general_case(state):
        losses, occurrence = state[2:]
        payload = pl.pallas_call(
            all_years_kernel,
            name="all_years",
            out_shape=jax.ShapeDtypeStruct((9 * shards, 128), jnp.float32),
            in_specs=[VMEM] * 2,
            out_specs=VMEM,
            compiler_params=compiler_params,
        )(losses, occurrence)
        arrived = lax.all_to_all(payload[:, None], "ev", split_axis=0, concat_axis=0, tiled=True)[:, 0]
        year_loss, _ = add_years(arrived, 9, True, "years_all")
        return year_loss, jnp.zeros((1, 1), jnp.int32), losses, occurrence

    year_loss, flag = add_years(arrived, 3, False, "years")
    state = lax.while_loop(lambda state: state[1][0, 0] > 0, general_case, (year_loss, flag, losses, occurrence))
    return state[0]


def solution(mesh):
    placed = (
        P("pol", "ev", None),
        P("pol", None),
        P("pol", None),
        P("pol"),
        P("pol"),
        P("pol"),
        P("pol"),
        P("pol"),
        P("ev", None),
    )
    return jax.shard_map(
        per_device, mesh=mesh, in_specs=placed, out_specs=P("pol", "ev"), check_vma=False
    )
```

```python
import functools

import jax
import jax.numpy as jnp
from jax import lax
from jax.experimental import pallas as pl
from jax.experimental.pallas import tpu as pltpu
from jax.sharding import PartitionSpec as P

SUMM_DEV = 4
YR_DEV = 1024
FIRST_POL = 5
FIRST_EV = 18
GROUP = 28
SLOT = 7
SLOTS = 16
NT = (((1,), (1,)), ((), ()))
VMEM = pl.BlockSpec(memory_space=pltpu.VMEM)


def two_terms(x):
    high = x.astype(jnp.bfloat16)
    return high, (x - high.astype(jnp.float32)).astype(jnp.bfloat16)


def local_kernel(
    ground_hbm,
    deduct_hbm,
    limit_hbm,
    owner_hbm,
    ded_hbm,
    lim_hbm,
    share_hbm,
    summ_hbm,
    years_hbm,
    out,
    out_years,
    ground,
    deduct,
    limit,
    owner,
    ded,
    lim,
    share,
    summ,
    years,
    terms,
    ids,
    params,
    sems,
):
    blocks = ground.shape[0]
    part = 4 * SLOT
    bounds = [(first, min(part, blocks - first)) for first in range(0, GROUP * SLOT, part)]
    small = [
        (years_hbm, years),
        (owner_hbm, owner),
        (ded_hbm, ded),
        (lim_hbm, lim),
        (share_hbm, share),
        (summ_hbm, summ),
    ]
    pairs = small + [(ground_hbm, ground), (deduct_hbm, deduct), (limit_hbm, limit)]
    copies = [pltpu.make_async_copy(source, target, sems.at[n]) for n, (source, target) in enumerate(pairs)]
    for copy in copies:
        copy.start()
    sub = lax.broadcasted_iota(jnp.int32, (8, 128), 0)
    lane = lax.broadcasted_iota(jnp.int32, (8, 128), 1)
    terms[:, 16 * SLOT :, :] = jnp.zeros((GROUP // 2, 128 - 16 * SLOT, 256), jnp.bfloat16)
    ids[...] = jnp.full((8, 256), -1.0, jnp.float32)
    params[...] = jnp.zeros((8, 128), jnp.float32)
    for copy in copies[: len(small)]:
        copy.wait()

    half_members, key, code, over = rank_years(years)
    ids[0:1, 0:blocks] = owner[...].astype(jnp.float32)
    block = lax.broadcasted_iota(jnp.int32, (32, 256), 1).astype(jnp.float32)
    at_row = jnp.floor((block + 0.5) * (1.0 / SLOT)) == lax.broadcasted_iota(jnp.int32, (32, 256), 0).astype(jnp.float32)
    policy = ids[0:1, :]
    upper = 256.0 * jnp.floor(policy * (1.0 / 256.0))
    left = jnp.concatenate([jnp.where(at_row, upper, 0.0), jnp.where(at_row, policy - upper, 0.0)], axis=0)
    block = lax.broadcasted_iota(jnp.int32, (256, 128), 0).astype(jnp.float32)
    block = block - SLOT * jnp.floor((block + 0.5) * (1.0 / SLOT))
    right = block + 16.0 * SLOT == lax.broadcasted_iota(jnp.int32, (256, 128), 1).astype(jnp.float32)
    columns = jnp.dot(
        left.astype(jnp.bfloat16), right.astype(jnp.float32).astype(jnp.bfloat16), preferred_element_type=jnp.float32
    )
    columns = columns[:32] + columns[32:]
    params[4:5, 0:64] = ded[...]
    params[5:6, 0:64] = lim[...]
    params[6:7, 0:64] = share[...]
    params[7:8, 0:64] = summ[...].astype(jnp.float32)
    own = params[...]

    for copy in copies[len(small) :]:
        copy.wait()
    out_years[...] = place_years(half_members, key, code, over)
    parity = lax.broadcasted_iota(jnp.int32, (8, 256), 0) % 2
    side = (lax.broadcasted_iota(jnp.int32, (8, 256), 1) // 64) % 2
    ones = (parity == side).astype(jnp.float32).astype(jnp.bfloat16)
    low_lanes = lax.broadcasted_iota(jnp.int32, (1, SLOT, 16, 128), 3) < 64
    tiles = [jnp.zeros((8, 128), jnp.float32) for _ in range(4)]
    for c, (first, count) in enumerate(bounds):
        lower = deduct[first : first + count].astype(jnp.float32)[:, None, :]
        upper = limit[first : first + count].astype(jnp.float32)[:, None, :]
        net = jnp.minimum(jnp.maximum(ground[first : first + count].astype(jnp.float32) - lower, 0.0), upper)
        net = net + pltpu.roll(net.reshape(16 * count, 128), 64, 1).reshape(net.shape)
        if count < part:
            net = jnp.concatenate([net, jnp.zeros((part - count, 16, 128), jnp.float32)], axis=0)
        net = net.reshape(2, 2, SLOT, 16, 128)
        both = jnp.where(low_lanes, net[:, 0], net[:, 1])
        for term, value in enumerate(two_terms(both)):
            terms[2 * c : 2 * c + 2, : 16 * SLOT, 128 * term : 128 * term + 128] = value.reshape(2, 16 * SLOT, 128)
        weights = terms[2 * c : 2 * c + 2].reshape(256, 256)
        sums = lax.dot_general(ones, weights, NT, preferred_element_type=jnp.float32)
        for n in (2 * c, 2 * c + 1):
            piece = sums[:, 128 * (n % 2) : 128 * (n % 2) + 128]
            tiles[n // 4] = jnp.where(sub // 2 == n % 4, piece, tiles[n // 4])
    tiles = [tiles[t] + columns[8 * t : 8 * t + 8] for t in range(4)]
    tiles[3] = jnp.where(sub < 4, tiles[3], own)
    for t in range(4):
        for k in range(out.shape[0]):
            out[k, 8 * t : 8 * t + 8, :] = tiles[t]


def rank_years(years):
    shards = 32
    year = jnp.concatenate([years[pl.ds(0, 8, stride=2), :], years[pl.ds(1, 8, stride=2), :]], axis=1).astype(jnp.float32)
    shard = jnp.floor(year * (1.0 / YR_DEV))
    code = year - YR_DEV * shard + 1.0
    shard_row = ((lax.broadcasted_iota(jnp.int32, (shards, 128), 0) + FIRST_EV) % shards).astype(jnp.float32)
    member = [(shard_row == shard[r : r + 1]).astype(jnp.float32) for r in range(8)]
    half = [jnp.concatenate([member[2 * j], member[2 * j + 1]], axis=1) for j in range(4)]
    first = lax.broadcasted_iota(jnp.int32, (256, 256), 0)
    second = lax.broadcasted_iota(jnp.int32, (256, 256), 1)
    before = ((first // 64 == second // 64) & (first < second)).astype(jnp.float32).astype(jnp.bfloat16)
    stacked = jnp.concatenate(half, axis=0)
    ahead = jnp.dot(stacked.astype(jnp.bfloat16), before, preferred_element_type=jnp.float32)
    rank = jnp.sum((stacked * ahead).reshape(4, shards, 256), axis=1)
    event = lax.broadcasted_iota(jnp.int32, (4, 256), 1) // 64 + 4 * lax.broadcasted_iota(jnp.int32, (4, 256), 0)
    key = 16.0 * rank + event.astype(jnp.float32)
    most = jnp.max(jnp.max(rank, axis=0, keepdims=True), axis=1, keepdims=True)
    return jnp.concatenate(half, axis=1).astype(jnp.bfloat16), key, code, jnp.where(most >= SLOTS, -1.0, 0.0)


def place_years(members, key, code, over):
    slot_row = lax.broadcasted_iota(jnp.int32, (16 * SLOTS, 256), 0).astype(jnp.float32)
    upper = jnp.floor(code * (1.0 / 16.0))
    sums = []
    for value in (upper, code - 16.0 * upper):
        right = []
        for j in range(4):
            flat = jnp.concatenate([value[2 * j : 2 * j + 1], value[2 * j + 1 : 2 * j + 2]], axis=1)
            right.append(jnp.where(slot_row == key[j : j + 1], flat, 0.0).astype(jnp.bfloat16))
        sums.append(lax.dot_general(members, jnp.concatenate(right, axis=1), NT, preferred_element_type=jnp.float32))
    return jnp.concatenate([16.0 * sums[0] + sums[1], jnp.broadcast_to(over, (8, 16 * SLOTS))], axis=0)


def policy_kernel(arrived, compact, out):
    owners = arrived.shape[0]
    width = owners * 32
    turned = arrived[...].reshape(width, 128).T
    row = lax.broadcasted_iota(jnp.int32, (1, width), 1) % 32
    high, low = two_terms(turned[: 16 * SLOT])
    local_row = lax.broadcasted_iota(jnp.int32, (64, width), 0).astype(jnp.float32).astype(jnp.bfloat16)
    one = jnp.ones((16, width), jnp.bfloat16)
    zero = jnp.zeros((16, width), jnp.bfloat16)
    left, right = [], []
    for i in range(SLOT):
        policy = jnp.where(row < GROUP, turned[16 * SLOT + i : 16 * SLOT + i + 1], -1.0)
        owner = jnp.floor(policy * (1.0 / 64.0))
        local = jnp.broadcast_to(policy - 64.0 * owner, (16, width)).astype(jnp.bfloat16)
        owner = jnp.broadcast_to(owner, (16, width)).astype(jnp.bfloat16)
        terms = [x[16 * i : 16 * i + 16] for x in (high, low)]
        masked = [jnp.where(owner == jnp.bfloat16(o), x, zero) for o in range(owners) for x in terms]
        left.append(jnp.concatenate(masked, axis=0))
        member = [jnp.where(local_row[16 * h : 16 * h + 16] == local, one, zero) for h in range(4)]
        right.append(jnp.concatenate(member, axis=0))
    total = lax.dot_general(
        jnp.concatenate(left, axis=1), jnp.concatenate(right, axis=1), NT, preferred_element_type=jnp.float32
    )

    own = lax.axis_index("pol") * SUMM_DEV
    losses = [jnp.zeros((16, 64), jnp.float32) for _ in range(SUMM_DEV)]
    for o in range(owners):
        policy_ground = total[32 * o : 32 * o + 16] + total[32 * o + 16 : 32 * o + 32]
        place = (o - FIRST_POL) % owners
        ded, lim, share, summ = [arrived[place, GROUP + n : GROUP + n + 1, 0:64] for n in range(4)]
        loss = share * jnp.minimum(jnp.maximum(policy_ground - ded, 0.0), lim)
        for k in range(SUMM_DEV):
            losses[k] = losses[k] + jnp.where(summ == (own + k).astype(jnp.float32), loss, 0.0)
    losses = jnp.concatenate(losses, axis=0)
    losses = jnp.concatenate([losses, jnp.zeros((128 - 16 * SUMM_DEV, 64), jnp.float32)], axis=0)
    ones = jnp.ones((8, 128), jnp.bfloat16)
    weights = jnp.concatenate(two_terms(losses), axis=1)
    sums = lax.dot_general(ones, weights, NT, preferred_element_type=jnp.float32)
    shards = out.shape[0] // 3
    lane = lax.broadcasted_iota(jnp.int32, (8, 128), 1)
    sums = jnp.where(lane < 16 * SUMM_DEV, sums, compact[shards : shards + 8, :128])
    for k in range(shards // 8):
        out[pl.ds(24 * k, 8, stride=3), :] = sums
    out[pl.ds(1, shards, stride=3), :] = compact[:shards, :128]
    out[pl.ds(2, shards, stride=3), :] = compact[:shards, 128:]


def all_years_kernel(losses, occurrence, out):
    turned = jnp.concatenate([occurrence[...].astype(jnp.float32).T, jnp.zeros((64, 112), jnp.float32)], axis=1)
    tiles = [turned[8 * r : 8 * r + 8] for r in range(8)]
    tiles = [pltpu.roll(t, 0, 1, stride=16, stride_axis=0) for t in tiles]
    lane = lax.broadcasted_iota(jnp.int32, (1, 128), 1)
    rows = [jnp.where(lane < 16 * SUMM_DEV, losses[0:1, :], 0.0)] + [jnp.sum(t, axis=0, keepdims=True) for t in tiles]
    nine = jnp.concatenate(rows, axis=0)
    for k in range(out.shape[0] // 9):
        out[9 * k : 9 * k + 9, :] = nine


def year_kernel(rows_per_source, whole, arrived, out, flag, uppers, lowers, spread, spare):
    sources = arrived.shape[0] // rows_per_source
    base = (lax.axis_index("ev") * YR_DEV).astype(jnp.float32) if whole else 1.0
    year = arrived[...] - base
    upper = jnp.floor(year * (1.0 / 128.0))
    uppers[...] = upper
    lowers[...] = year - 128.0 * upper

    first = arrived[pl.ds(0, sources, stride=rows_per_source), :]
    flag[0, 0] = (jnp.min(first) < 0.0).astype(jnp.int32)
    high, low = two_terms(first)
    lane = lax.broadcasted_iota(jnp.int32, (128, 128), 1)
    sub = lax.broadcasted_iota(jnp.int32, (128, 128), 0)
    repeat = jnp.concatenate(
        [(sub == lane % 16 + 16 * k).astype(jnp.float32).astype(jnp.bfloat16) for k in range(SUMM_DEV)], axis=1
    )
    spread[...] = jnp.dot(jnp.concatenate([high, low], axis=0), repeat, preferred_element_type=jnp.float32)

    row = sub.astype(jnp.float32).astype(jnp.bfloat16)
    upper_row = (lax.broadcasted_iota(jnp.int32, (16, 128), 0) % 8).astype(jnp.float32).astype(jnp.bfloat16)
    one = jnp.ones((16, 128), jnp.bfloat16)
    zero = jnp.zeros((16, 128), jnp.bfloat16)

    def step(source, total):
        losses = []
        for term in range(2):
            values = spread[pl.ds(term * sources + source, 1), :]
            for k in range(0, SUMM_DEV, 2):
                pair = [jnp.broadcast_to(values[:, 128 * (k + i) : 128 * (k + i) + 128], (8, 128)) for i in range(2)]
                losses.append(jnp.concatenate(pair, axis=0).astype(jnp.bfloat16))
        left, right = [], []
        for r in range(1, rows_per_source):
            at = pl.ds(rows_per_source * source + r, 1)
            upper = jnp.broadcast_to(uppers[at, :], (16, 128)).astype(jnp.bfloat16)
            lower = jnp.broadcast_to(lowers[at, :], (16, 128)).astype(jnp.bfloat16)
            match = upper == upper_row
            right.append(jnp.concatenate([jnp.where(match, x, zero) for x in losses], axis=0))
            left.append(
                jnp.concatenate([jnp.where(row[16 * h : 16 * h + 16] == lower, one, zero) for h in range(8)], axis=0)
            )
        return total + lax.dot_general(
            jnp.concatenate(left, axis=1), jnp.concatenate(right, axis=1), NT, preferred_element_type=jnp.float32
        )

    total = lax.fori_loop(0, sources, step, jnp.zeros((128, 64), jnp.float32), unroll=32 if rows_per_source == 3 else 8).T
    spare[...] = total[:32] + total[32:]
    for h in range(8):
        out[:, 128 * h : 128 * h + 128] = spare[pl.ds(h, SUMM_DEV, stride=8), :]


def per_device(
    ground_up,
    loc_deductible,
    loc_limit,
    block_policy,
    policy_deductible,
    policy_limit,
    policy_share,
    policy_summary,
    occurrence,
):
    owners = lax.axis_size("pol")
    shards = lax.axis_size("ev")
    compiler_params = pltpu.CompilerParams(vmem_limit_bytes=32 * 1024 * 1024)
    payload, compact = pl.pallas_call(
        local_kernel,
        name="local",
        out_shape=(
            jax.ShapeDtypeStruct((owners, 32, 128), jnp.float32),
            jax.ShapeDtypeStruct((shards + 8, 16 * SLOTS), jnp.float32),
        ),
        in_specs=[pl.BlockSpec(memory_space=pltpu.HBM)] * 9,
        out_specs=(VMEM, VMEM),
        scratch_shapes=[
            pltpu.VMEM(ground_up.shape, jnp.bfloat16),
            pltpu.VMEM(loc_deductible.shape, jnp.bfloat16),
            pltpu.VMEM(loc_limit.shape, jnp.bfloat16),
            pltpu.VMEM((1, block_policy.shape[0]), jnp.int32),
            pltpu.VMEM((1, 64), jnp.float32),
            pltpu.VMEM((1, 64), jnp.float32),
            pltpu.VMEM((1, 64), jnp.float32),
            pltpu.VMEM((1, 64), jnp.int32),
            pltpu.VMEM(occurrence.shape, jnp.int32),
            pltpu.VMEM((GROUP // 2, 128, 256), jnp.bfloat16),
            pltpu.VMEM((8, 256), jnp.float32),
            pltpu.VMEM((8, 128), jnp.float32),
            pltpu.SemaphoreType.DMA((9,)),
        ],
        compiler_params=compiler_params,
    )(
        pltpu.with_memory_space_constraint(ground_up, pltpu.HBM),
        pltpu.with_memory_space_constraint(loc_deductible, pltpu.HBM),
        pltpu.with_memory_space_constraint(loc_limit, pltpu.HBM),
        pltpu.with_memory_space_constraint(block_policy[None], pltpu.HBM),
        pltpu.with_memory_space_constraint(policy_deductible[None], pltpu.HBM),
        pltpu.with_memory_space_constraint(policy_limit[None], pltpu.HBM),
        pltpu.with_memory_space_constraint(policy_share[None], pltpu.HBM),
        pltpu.with_memory_space_constraint(policy_summary[None], pltpu.HBM),
        pltpu.with_memory_space_constraint(occurrence, pltpu.HBM),
    )
    order = [[(i + FIRST_POL) % owners for i in range(owners)]]
    arrived = lax.all_to_all(payload, "pol", split_axis=0, concat_axis=0, axis_index_groups=order, tiled=True)
    losses = pl.pallas_call(
        policy_kernel,
        name="policies",
        out_shape=jax.ShapeDtypeStruct((3 * shards, 128), jnp.float32),
        in_specs=[VMEM] * 2,
        out_specs=VMEM,
        compiler_params=compiler_params,
    )(arrived, compact)
    order = [[(i + FIRST_EV) % shards for i in range(shards)]]
    arrived = lax.all_to_all(
        losses.reshape(shards, 1, 3 * 128), "ev", split_axis=0, concat_axis=0, axis_index_groups=order, tiled=True
    )
    arrived = arrived.reshape(3 * shards, 128)

    def add_years(arrived, rows_per_source, whole, name):
        return pl.pallas_call(
            functools.partial(year_kernel, rows_per_source, whole),
            name=name,
            out_shape=(
                jax.ShapeDtypeStruct((SUMM_DEV, YR_DEV), jnp.float32),
                jax.ShapeDtypeStruct((1, 1), jnp.int32),
            ),
            in_specs=[VMEM],
            out_specs=(VMEM, pl.BlockSpec(memory_space=pltpu.SMEM)),
            scratch_shapes=[
                pltpu.VMEM((rows_per_source * shards, 128), jnp.float32),
                pltpu.VMEM((rows_per_source * shards, 128), jnp.float32),
                pltpu.VMEM((2 * shards, 128 * SUMM_DEV), jnp.float32),
                pltpu.VMEM((32, 128), jnp.float32),
            ],
            compiler_params=compiler_params,
        )(arrived)

    def general_case(state):
        losses, occurrence = state[2:]
        payload = pl.pallas_call(
            all_years_kernel,
            name="all_years",
            out_shape=jax.ShapeDtypeStruct((9 * shards, 128), jnp.float32),
            in_specs=[VMEM] * 2,
            out_specs=VMEM,
            compiler_params=compiler_params,
        )(losses, occurrence)
        arrived = lax.all_to_all(payload[:, None], "ev", split_axis=0, concat_axis=0, tiled=True)[:, 0]
        year_loss, _ = add_years(arrived, 9, True, "years_all")
        return year_loss, jnp.zeros((1, 1), jnp.int32), losses, occurrence

    year_loss, flag = add_years(arrived, 3, False, "years")
    state = lax.while_loop(lambda state: state[1][0, 0] > 0, general_case, (year_loss, flag, losses, occurrence))
    return state[0]


def solution(mesh):
    placed = (
        P("pol", "ev", None),
        P("pol", None),
        P("pol", None),
        P("pol"),
        P("pol"),
        P("pol"),
        P("pol"),
        P("pol"),
        P("ev", None),
    )
    return jax.shard_map(
        per_device, mesh=mesh, in_specs=placed, out_specs=P("pol", "ev"), check_vma=False
    )
```

```python
import functools

import jax
import jax.numpy as jnp
from jax import lax
from jax.experimental import pallas as pl
from jax.experimental.pallas import tpu as pltpu
from jax.sharding import PartitionSpec as P

SUMM_DEV = 4
YR_DEV = 1024
FIRST_POL = 5
FIRST_EV = 18
GROUP = 28
SLOT = 7
SLOTS = 16
NT = (((1,), (1,)), ((), ()))
VMEM = pl.BlockSpec(memory_space=pltpu.VMEM)


def two_terms(x):
    high = x.astype(jnp.bfloat16)
    return high, (x - high.astype(jnp.float32)).astype(jnp.bfloat16)


def local_kernel(
    ground_hbm,
    deduct_hbm,
    limit_hbm,
    owner_hbm,
    ded_hbm,
    lim_hbm,
    share_hbm,
    summ_hbm,
    years_hbm,
    out,
    out_years,
    ground,
    deduct,
    limit,
    owner,
    ded,
    lim,
    share,
    summ,
    years,
    terms,
    ids,
    params,
    sems,
):
    blocks = ground.shape[0]
    part = 4 * SLOT
    bounds = [(first, min(part, blocks - first)) for first in range(0, GROUP * SLOT, part)]
    small = [
        (years_hbm, years),
        (owner_hbm, owner),
        (ded_hbm, ded),
        (lim_hbm, lim),
        (share_hbm, share),
        (summ_hbm, summ),
    ]
    pairs = small + [(ground_hbm, ground), (deduct_hbm, deduct), (limit_hbm, limit)]
    copies = [pltpu.make_async_copy(source, target, sems.at[n]) for n, (source, target) in enumerate(pairs)]
    for copy in copies:
        copy.start()
    sub = lax.broadcasted_iota(jnp.int32, (8, 128), 0)
    lane = lax.broadcasted_iota(jnp.int32, (8, 128), 1)
    terms[:, 16 * SLOT :, :] = jnp.zeros((GROUP // 2, 128 - 16 * SLOT, 256), jnp.bfloat16)
    ids[...] = jnp.full((8, 256), -1.0, jnp.float32)
    params[...] = jnp.zeros((8, 128), jnp.float32)
    for copy in copies[: len(small)]:
        copy.wait()

    half_members, key, code, over = rank_years(years)
    ids[0:1, 0:blocks] = owner[...].astype(jnp.float32)
    block = lax.broadcasted_iota(jnp.int32, (32, 256), 1).astype(jnp.float32)
    at_row = jnp.floor((block + 0.5) * (1.0 / SLOT)) == lax.broadcasted_iota(jnp.int32, (32, 256), 0).astype(jnp.float32)
    policy = ids[0:1, :]
    upper = 256.0 * jnp.floor(policy * (1.0 / 256.0))
    left = jnp.concatenate([jnp.where(at_row, upper, 0.0), jnp.where(at_row, policy - upper, 0.0)], axis=0)
    block = lax.broadcasted_iota(jnp.int32, (256, 128), 0).astype(jnp.float32)
    block = block - SLOT * jnp.floor((block + 0.5) * (1.0 / SLOT))
    right = block + 16.0 * SLOT == lax.broadcasted_iota(jnp.int32, (256, 128), 1).astype(jnp.float32)
    columns = jnp.dot(
        left.astype(jnp.bfloat16), right.astype(jnp.float32).astype(jnp.bfloat16), preferred_element_type=jnp.float32
    )
    columns = columns[:32] + columns[32:]
    params[4:5, 0:64] = ded[...]
    params[5:6, 0:64] = lim[...]
    params[6:7, 0:64] = share[...]
    params[7:8, 0:64] = summ[...].astype(jnp.float32)
    own = params[...]

    for copy in copies[len(small) :]:
        copy.wait()
    out_years[...] = place_years(half_members, key, code, over)
    parity = lax.broadcasted_iota(jnp.int32, (8, 256), 0) % 2
    side = (lax.broadcasted_iota(jnp.int32, (8, 256), 1) // 64) % 2
    ones = (parity == side).astype(jnp.float32).astype(jnp.bfloat16)
    low_lanes = lax.broadcasted_iota(jnp.int32, (1, SLOT, 16, 128), 3) < 64
    tiles = [jnp.zeros((8, 128), jnp.float32) for _ in range(4)]
    for c, (first, count) in enumerate(bounds):
        lower = deduct[first : first + count].astype(jnp.float32)[:, None, :]
        upper = limit[first : first + count].astype(jnp.float32)[:, None, :]
        net = jnp.minimum(jnp.maximum(ground[first : first + count].astype(jnp.float32) - lower, 0.0), upper)
        net = net + pltpu.roll(net.reshape(16 * count, 128), 64, 1).reshape(net.shape)
        if count < part:
            net = jnp.concatenate([net, jnp.zeros((part - count, 16, 128), jnp.float32)], axis=0)
        net = net.reshape(2, 2, SLOT, 16, 128)
        both = jnp.where(low_lanes, net[:, 0], net[:, 1])
        for term, value in enumerate(two_terms(both)):
            terms[2 * c : 2 * c + 2, : 16 * SLOT, 128 * term : 128 * term + 128] = value.reshape(2, 16 * SLOT, 128)
        weights = terms[2 * c : 2 * c + 2].reshape(256, 256)
        sums = lax.dot_general(ones, weights, NT, preferred_element_type=jnp.float32)
        for n in (2 * c, 2 * c + 1):
            piece = sums[:, 128 * (n % 2) : 128 * (n % 2) + 128]
            tiles[n // 4] = jnp.where(sub // 2 == n % 4, piece, tiles[n // 4])
    tiles = [tiles[t] + columns[8 * t : 8 * t + 8] for t in range(4)]
    tiles[3] = jnp.where(sub < 4, tiles[3], own)
    for t in range(4):
        for k in range(out.shape[0]):
            out[k, 8 * t : 8 * t + 8, :] = tiles[t]


def rank_years(years):
    shards = 32
    year = jnp.concatenate([years[pl.ds(0, 8, stride=2), :], years[pl.ds(1, 8, stride=2), :]], axis=1).astype(jnp.float32)
    shard = jnp.floor(year * (1.0 / YR_DEV))
    code = year - YR_DEV * shard + 1.0
    shard_row = ((lax.broadcasted_iota(jnp.int32, (shards, 128), 0) + FIRST_EV) % shards).astype(jnp.float32)
    member = [(shard_row == shard[r : r + 1]).astype(jnp.float32) for r in range(8)]
    half = [jnp.concatenate([member[2 * j], member[2 * j + 1]], axis=1) for j in range(4)]
    first = lax.broadcasted_iota(jnp.int32, (256, 256), 0)
    second = lax.broadcasted_iota(jnp.int32, (256, 256), 1)
    before = ((first // 64 == second // 64) & (first < second)).astype(jnp.float32).astype(jnp.bfloat16)
    stacked = jnp.concatenate(half, axis=0)
    ahead = jnp.dot(stacked.astype(jnp.bfloat16), before, preferred_element_type=jnp.float32)
    rank = jnp.sum((stacked * ahead).reshape(4, shards, 256), axis=1)
    event = lax.broadcasted_iota(jnp.int32, (4, 256), 1) // 64 + 4 * lax.broadcasted_iota(jnp.int32, (4, 256), 0)
    key = 16.0 * rank + event.astype(jnp.float32)
    most = jnp.max(jnp.max(rank, axis=0, keepdims=True), axis=1, keepdims=True)
    return jnp.concatenate(half, axis=1).astype(jnp.bfloat16), key, code, jnp.where(most >= SLOTS, -1.0, 0.0)


def place_years(members, key, code, over):
    slot_row = lax.broadcasted_iota(jnp.int32, (16 * SLOTS, 256), 0).astype(jnp.float32)
    upper = jnp.floor(code * (1.0 / 16.0))
    sums = []
    for value in (upper, code - 16.0 * upper):
        right = []
        for j in range(4):
            flat = jnp.concatenate([value[2 * j : 2 * j + 1], value[2 * j + 1 : 2 * j + 2]], axis=1)
            right.append(jnp.where(slot_row == key[j : j + 1], flat, 0.0).astype(jnp.bfloat16))
        sums.append(lax.dot_general(members, jnp.concatenate(right, axis=1), NT, preferred_element_type=jnp.float32))
    return jnp.concatenate([16.0 * sums[0] + sums[1], jnp.broadcast_to(over, (8, 16 * SLOTS))], axis=0)


def policy_kernel(arrived, compact, out):
    owners = arrived.shape[0]
    width = owners * 32
    turned = arrived[...].reshape(width, 128).T
    row = lax.broadcasted_iota(jnp.int32, (1, width), 1) % 32
    high, low = two_terms(turned[: 16 * SLOT])
    local_row = lax.broadcasted_iota(jnp.int32, (64, width), 0).astype(jnp.float32).astype(jnp.bfloat16)
    one = jnp.ones((16, width), jnp.bfloat16)
    zero = jnp.zeros((16, width), jnp.bfloat16)
    left, right = [], []
    for i in range(SLOT):
        policy = jnp.where(row < GROUP, turned[16 * SLOT + i : 16 * SLOT + i + 1], -1.0)
        owner = jnp.floor(policy * (1.0 / 64.0))
        local = jnp.broadcast_to(policy - 64.0 * owner, (16, width)).astype(jnp.bfloat16)
        owner = jnp.broadcast_to(owner, (16, width)).astype(jnp.bfloat16)
        terms = [x[16 * i : 16 * i + 16] for x in (high, low)]
        masked = [jnp.where(owner == jnp.bfloat16(o), x, zero) for o in range(owners) for x in terms]
        left.append(jnp.concatenate(masked, axis=0))
        member = [jnp.where(local_row[16 * h : 16 * h + 16] == local, one, zero) for h in range(4)]
        right.append(jnp.concatenate(member, axis=0))
    total = lax.dot_general(
        jnp.concatenate(left, axis=1), jnp.concatenate(right, axis=1), NT, preferred_element_type=jnp.float32
    )

    own = lax.axis_index("pol") * SUMM_DEV
    losses = [jnp.zeros((16, 64), jnp.float32) for _ in range(SUMM_DEV)]
    for o in range(owners):
        policy_ground = total[32 * o : 32 * o + 16] + total[32 * o + 16 : 32 * o + 32]
        place = (o - FIRST_POL) % owners
        ded, lim, share, summ = [arrived[place, GROUP + n : GROUP + n + 1, 0:64] for n in range(4)]
        loss = share * jnp.minimum(jnp.maximum(policy_ground - ded, 0.0), lim)
        for k in range(SUMM_DEV):
            losses[k] = losses[k] + jnp.where(summ == (own + k).astype(jnp.float32), loss, 0.0)
    losses = jnp.concatenate(losses, axis=0)
    losses = jnp.concatenate([losses, jnp.zeros((128 - 16 * SUMM_DEV, 64), jnp.float32)], axis=0)
    ones = jnp.ones((8, 128), jnp.bfloat16)
    weights = jnp.concatenate(two_terms(losses), axis=1)
    sums = lax.dot_general(ones, weights, NT, preferred_element_type=jnp.float32)
    shards = out.shape[0] // 3
    lane = lax.broadcasted_iota(jnp.int32, (8, 128), 1)
    sums = jnp.where(lane < 16 * SUMM_DEV, sums, compact[shards : shards + 8, :128])
    for k in range(shards // 8):
        out[pl.ds(24 * k, 8, stride=3), :] = sums
    out[pl.ds(1, shards, stride=3), :] = compact[:shards, :128]
    out[pl.ds(2, shards, stride=3), :] = compact[:shards, 128:]


def all_years_kernel(losses, occurrence, out):
    turned = jnp.concatenate([occurrence[...].astype(jnp.float32).T, jnp.zeros((64, 112), jnp.float32)], axis=1)
    tiles = [turned[8 * r : 8 * r + 8] for r in range(8)]
    tiles = [pltpu.roll(t, 0, 1, stride=16, stride_axis=0) for t in tiles]
    lane = lax.broadcasted_iota(jnp.int32, (1, 128), 1)
    rows = [jnp.where(lane < 16 * SUMM_DEV, losses[0:1, :], 0.0)] + [jnp.sum(t, axis=0, keepdims=True) for t in tiles]
    nine = jnp.concatenate(rows, axis=0)
    for k in range(out.shape[0] // 9):
        out[9 * k : 9 * k + 9, :] = nine


def year_kernel(rows_per_source, whole, arrived, out, flag, uppers, lowers, spread, spare):
    sources = arrived.shape[0] // rows_per_source
    base = (lax.axis_index("ev") * YR_DEV).astype(jnp.float32) if whole else 1.0
    year = arrived[...] - base
    upper = jnp.floor(year * (1.0 / 128.0))
    uppers[...] = upper
    lowers[...] = year - 128.0 * upper

    first = arrived[pl.ds(0, sources, stride=rows_per_source), :]
    flag[0, 0] = (jnp.min(first) < 0.0).astype(jnp.int32)
    high, low = two_terms(first)
    lane = lax.broadcasted_iota(jnp.int32, (128, 128), 1)
    sub = lax.broadcasted_iota(jnp.int32, (128, 128), 0)
    repeat = jnp.concatenate(
        [(sub == lane % 16 + 16 * k).astype(jnp.float32).astype(jnp.bfloat16) for k in range(SUMM_DEV)], axis=1
    )
    spread[...] = jnp.dot(jnp.concatenate([high, low], axis=0), repeat, preferred_element_type=jnp.float32)

    row = sub.astype(jnp.float32).astype(jnp.bfloat16)
    upper_row = (lax.broadcasted_iota(jnp.int32, (16, 128), 0) % 8).astype(jnp.float32).astype(jnp.bfloat16)
    one = jnp.ones((16, 128), jnp.bfloat16)
    zero = jnp.zeros((16, 128), jnp.bfloat16)

    together = 8 // (rows_per_source - 1)

    def step(group, total):
        left, right = [], []
        for source in [together * group + n for n in range(together)]:
            losses = []
            for term in range(2):
                values = spread[pl.ds(term * sources + source, 1), :]
                for k in range(0, SUMM_DEV, 2):
                    pair = [
                        jnp.broadcast_to(values[:, 128 * (k + i) : 128 * (k + i) + 128], (8, 128)) for i in range(2)
                    ]
                    losses.append(jnp.concatenate(pair, axis=0).astype(jnp.bfloat16))
            for r in range(1, rows_per_source):
                at = pl.ds(rows_per_source * source + r, 1)
                upper = jnp.broadcast_to(uppers[at, :], (16, 128)).astype(jnp.bfloat16)
                lower = jnp.broadcast_to(lowers[at, :], (16, 128)).astype(jnp.bfloat16)
                match = upper == upper_row
                right.append(jnp.concatenate([jnp.where(match, x, zero) for x in losses], axis=0))
                left.append(
                    jnp.concatenate(
                        [jnp.where(row[16 * h : 16 * h + 16] == lower, one, zero) for h in range(8)], axis=0
                    )
                )
        return total + lax.dot_general(
            jnp.concatenate(left, axis=1), jnp.concatenate(right, axis=1), NT, preferred_element_type=jnp.float32
        )

    total = lax.fori_loop(0, sources // together, step, jnp.zeros((128, 64), jnp.float32), unroll=8).T
    spare[...] = total[:32] + total[32:]
    for h in range(8):
        out[:, 128 * h : 128 * h + 128] = spare[pl.ds(h, SUMM_DEV, stride=8), :]


def per_device(
    ground_up,
    loc_deductible,
    loc_limit,
    block_policy,
    policy_deductible,
    policy_limit,
    policy_share,
    policy_summary,
    occurrence,
):
    owners = lax.axis_size("pol")
    shards = lax.axis_size("ev")
    compiler_params = pltpu.CompilerParams(vmem_limit_bytes=32 * 1024 * 1024)
    payload, compact = pl.pallas_call(
        local_kernel,
        name="local",
        out_shape=(
            jax.ShapeDtypeStruct((owners, 32, 128), jnp.float32),
            jax.ShapeDtypeStruct((shards + 8, 16 * SLOTS), jnp.float32),
        ),
        in_specs=[pl.BlockSpec(memory_space=pltpu.HBM)] * 9,
        out_specs=(VMEM, VMEM),
        scratch_shapes=[
            pltpu.VMEM(ground_up.shape, jnp.bfloat16),
            pltpu.VMEM(loc_deductible.shape, jnp.bfloat16),
            pltpu.VMEM(loc_limit.shape, jnp.bfloat16),
            pltpu.VMEM((1, block_policy.shape[0]), jnp.int32),
            pltpu.VMEM((1, 64), jnp.float32),
            pltpu.VMEM((1, 64), jnp.float32),
            pltpu.VMEM((1, 64), jnp.float32),
            pltpu.VMEM((1, 64), jnp.int32),
            pltpu.VMEM(occurrence.shape, jnp.int32),
            pltpu.VMEM((GROUP // 2, 128, 256), jnp.bfloat16),
            pltpu.VMEM((8, 256), jnp.float32),
            pltpu.VMEM((8, 128), jnp.float32),
            pltpu.SemaphoreType.DMA((9,)),
        ],
        compiler_params=compiler_params,
    )(
        pltpu.with_memory_space_constraint(ground_up, pltpu.HBM),
        pltpu.with_memory_space_constraint(loc_deductible, pltpu.HBM),
        pltpu.with_memory_space_constraint(loc_limit, pltpu.HBM),
        pltpu.with_memory_space_constraint(block_policy[None], pltpu.HBM),
        pltpu.with_memory_space_constraint(policy_deductible[None], pltpu.HBM),
        pltpu.with_memory_space_constraint(policy_limit[None], pltpu.HBM),
        pltpu.with_memory_space_constraint(policy_share[None], pltpu.HBM),
        pltpu.with_memory_space_constraint(policy_summary[None], pltpu.HBM),
        pltpu.with_memory_space_constraint(occurrence, pltpu.HBM),
    )
    order = [[(i + FIRST_POL) % owners for i in range(owners)]]
    arrived = lax.all_to_all(payload, "pol", split_axis=0, concat_axis=0, axis_index_groups=order, tiled=True)
    losses = pl.pallas_call(
        policy_kernel,
        name="policies",
        out_shape=jax.ShapeDtypeStruct((3 * shards, 128), jnp.float32),
        in_specs=[VMEM] * 2,
        out_specs=VMEM,
        compiler_params=compiler_params,
    )(arrived, compact)
    order = [[(i + FIRST_EV) % shards for i in range(shards)]]
    arrived = lax.all_to_all(
        losses.reshape(shards, 1, 3 * 128), "ev", split_axis=0, concat_axis=0, axis_index_groups=order, tiled=True
    )
    arrived = arrived.reshape(3 * shards, 128)

    def add_years(arrived, rows_per_source, whole, name):
        return pl.pallas_call(
            functools.partial(year_kernel, rows_per_source, whole),
            name=name,
            out_shape=(
                jax.ShapeDtypeStruct((SUMM_DEV, YR_DEV), jnp.float32),
                jax.ShapeDtypeStruct((1, 1), jnp.int32),
            ),
            in_specs=[VMEM],
            out_specs=(VMEM, pl.BlockSpec(memory_space=pltpu.SMEM)),
            scratch_shapes=[
                pltpu.VMEM((rows_per_source * shards, 128), jnp.float32),
                pltpu.VMEM((rows_per_source * shards, 128), jnp.float32),
                pltpu.VMEM((2 * shards, 128 * SUMM_DEV), jnp.float32),
                pltpu.VMEM((32, 128), jnp.float32),
            ],
            compiler_params=compiler_params,
        )(arrived)

    def general_case(state):
        losses, occurrence = state[2:]
        payload = pl.pallas_call(
            all_years_kernel,
            name="all_years",
            out_shape=jax.ShapeDtypeStruct((9 * shards, 128), jnp.float32),
            in_specs=[VMEM] * 2,
            out_specs=VMEM,
            compiler_params=compiler_params,
        )(losses, occurrence)
        arrived = lax.all_to_all(payload[:, None], "ev", split_axis=0, concat_axis=0, tiled=True)[:, 0]
        year_loss, _ = add_years(arrived, 9, True, "years_all")
        return year_loss, jnp.zeros((1, 1), jnp.int32), losses, occurrence

    year_loss, flag = add_years(arrived, 3, False, "years")
    state = lax.while_loop(lambda state: state[1][0, 0] > 0, general_case, (year_loss, flag, losses, occurrence))
    return state[0]


def solution(mesh):
    placed = (
        P("pol", "ev", None),
        P("pol", None),
        P("pol", None),
        P("pol"),
        P("pol"),
        P("pol"),
        P("pol"),
        P("pol"),
        P("ev", None),
    )
    return jax.shard_map(
        per_device, mesh=mesh, in_specs=placed, out_specs=P("pol", "ev"), check_vma=False
    )
```
